128 devices in a mesh: col: 8 (over x_lo, y), row: 16 (over x_hi, z, core).
Axes of the slice: x: 4 (x_hi: 2, x_lo: 2; x = x_hi * 2 + x_lo), y: 4, z: 4, core: 2. Of those that a mesh axis runs over, the one named last changes fastest.
Arguments:
- sigma_ret: float32 [16384, 16384], P('col', 'row'), may hold values from -0.0625 to 0.0625
- sigma_less: float32 [16384, 16384], P('col', 'row'), may hold values from -0.046875 to 0.046875
- green_less: float32 [16384, 1024], P('row', 'col'), may hold values from -6 to 6
- green_ret: float32 [1024, 16384], P(('col', 'row')), may hold values from -6 to 6
Outputs:
- collision: float32 [16384, 1024], P(('col', 'row'))
The draws below stay inside these ranges and needn't reach their ends.
All inputs are finite; a program needn't handle non-finite values.
Results may differ from the reference program's by a relative error of at most 0.00007.
Values sent between devices are 32-bit elements; how exact they have to be, the bound alone decides.
A program may use at most 128 MiB of HBM per device.

```python
import jax
import jax.numpy as jnp
from jax import lax

M = 16384
W = 1024


def raised(values, key, source, target, blocks, factor):
    owner, partner = [(jnp.arange(values.shape[position]) // (values.shape[position] // blocks)).reshape([-1 if axis == position else 1 for axis in range(values.ndim)]) for position in (source, target)]
    chosen = jax.random.permutation(key, blocks)[partner]
    strong = (owner == chosen) | (owner == (partner + blocks // 2) % blocks)
    return jnp.where(strong, factor * values, values)


def steps_of(rng, extent, pieces, smallest, high):
    factor_of, own = 1.0, jax.random.fold_in(rng, 6)
    for dim, shards_of in pieces:
        heights = jnp.exp(jax.random.uniform(jax.random.fold_in(own, dim), (shards_of,), jnp.float32, smallest / len(pieces), high / len(pieces)))
        factor_of = factor_of * jnp.repeat(heights, extent[dim] // shards_of).reshape([-1 if axis == dim else 1 for axis in range(len(extent))])
    return factor_of


def noise(rng, shape, spread, bound, pieces=(), held_as=jnp.bfloat16):
    drawn = jax.random.normal(rng, shape, jnp.float32) * spread
    if len(pieces) > 0:
        drawn = steps_of(rng, shape, pieces, -0.22, 0.18) * drawn
    return jnp.clip(drawn, min=-bound, max=bound).astype(held_as)


def noise_with(own_key, shape, width, bound, pieces, heavy, kind=jnp.bfloat16):
    result = width * jax.random.normal(own_key, shape, jnp.float32)
    if pieces:
        result = result * steps_of(own_key, shape, pieces, -0.22, 0.18)
    return jnp.clip(raised(result, jax.random.fold_in(own_key, 3), *heavy), -bound, bound).astype(kind)


def setup_inputs(seed: int = 0) -> dict:
    key_of = jax.random.split(jax.random.key(seed), 5)
    sigma_ret = noise_with(key_of[0], (M, M), M ** -0.5, 0.0625, ((0, 8), (1, 16)), (1, 0, 16, 2.0), jnp.float32)
    sigma_less = noise(key_of[1], (M, M), M ** -0.5, 0.046875, ((0, 8), (1, 16)), jnp.float32)
    green_less = noise(key_of[2], (M, W), 1.0, 6.0, ((0, 16), (1, 8)), jnp.float32)
    green_ret = noise(key_of[3], (W, M), 1.0, 6.0, ((0, 128),), jnp.float32)
    return dict(sigma_ret=sigma_ret, sigma_less=sigma_less, green_less=green_less, green_ret=green_ret)


def reference(sigma_ret, sigma_less, green_less, green_ret):
    highest = lax.Precision.HIGHEST
    green_adv = jnp.transpose(green_ret)
    first_term = jnp.dot(sigma_ret, green_less, precision=highest, preferred_element_type=jnp.float32)
    second_term = jnp.dot(sigma_less, green_adv, precision=highest, preferred_element_type=jnp.float32)
    return first_term + second_term
```

```python
import jax
import jax.numpy as jnp
from jax import lax
from jax.experimental import pallas as pl
from jax.experimental.pallas import tpu as pltpu
from jax.sharding import PartitionSpec as P

MESH = pl.DeviceIdType.MESH
F32 = jnp.float32
BF16 = jnp.bfloat16

NY, NZ = 4, 4
COLS, ROWS = 8, 16

DY = (0, 1, 3, 2)
LESSER, ADVANCED = 0, 1
DZ = (2, 1, 3, 0)
TILE = 512
AHEAD = 8


def kernel(
    sigma_ret, sigma_less, green_less, green_ret, out,
    lesser, advanced, mirror, high, low, stage, lesser_w, advanced_w,
    part, part_in, z_in, x_out, x_in, total,
    load_sem, stage_sem, a2a_send, a2a_recv, send, recv,
    chip_send, chip_recv, z_send, z_recv, x_send, x_recv, out_sem,
):
    col, row = lax.axis_index("col"), lax.axis_index("row")
    x_lo, y = col // NY, col % NY
    x_hi, z, core = row // (2 * NZ), (row // 2) % NZ, row % 2

    def at_col(dx, dy):
        return (((x_lo + dx) % 2) * NY + (y + dy) % NY, row)

    def at_row(dx, dz, dcore):
        return (col, ((x_hi + dx) % 2) * 2 * NZ + ((z + dz) % NZ) * 2 + (core + dcore) % 2)

    y_up, y_down, x_pair = at_col(0, 1), at_col(0, NY - 1), at_col(1, 0)

    load_lesser = pltpu.make_async_copy(green_less, lesser.at[0], load_sem.at[0])
    load_mirror = pltpu.make_async_copy(green_ret, mirror, load_sem.at[1])
    load_lesser.start()
    load_mirror.start()

    def stage_copy(matrix, source, t):
        half, p = t // 8, t % 8
        q = p // 2
        dz = jnp.where(q == 0, DZ[0], jnp.where(q == 1, DZ[1], jnp.where(q == 2, DZ[2], DZ[3])))
        block = at_row(p % 2, dz, 1 - half)[1]
        return pltpu.make_async_copy(
            source.at[pl.ds(pl.multiple_of(block * 128, 128), 128), :],
            stage.at[t % AHEAD],
            stage_sem.at[t % AHEAD],
        )

    for t in range(AHEAD):
        stage_copy(0, sigma_ret, t).start()

    barrier = pltpu.get_barrier_semaphore()
    peers = [y_up, y_down, x_pair] + [(col, (row + d) % ROWS) for d in range(1, ROWS)]
    for peer in peers:
        pl.semaphore_signal(barrier, inc=1, device_id=peer, device_id_type=MESH)
    pl.semaphore_wait(barrier, len(peers))

    def remote(src, dst, send_sem, recv_sem, device):
        return pltpu.make_async_remote_copy(
            src_ref=src, dst_ref=dst, send_sem=send_sem, recv_sem=recv_sem,
            device_id=device, device_id_type=MESH,
        )

    load_mirror.wait()
    exchanges = []
    mine = pl.ds(pl.multiple_of(row * 8, 8), 8)
    for d in range(1, ROWS):
        target = (row + d) % ROWS
        exchanges.append(remote(
            mirror.at[:, pl.ds(pl.multiple_of(target * 1024, 1024), 1024)],
            advanced.at[0, mine, :],
            a2a_send.at[d - 1], a2a_recv.at[d - 1], (col, target),
        ))
    own_piece = pltpu.make_async_copy(
        mirror.at[:, pl.ds(pl.multiple_of(row * 1024, 1024), 1024)],
        advanced.at[0, mine, :], load_sem.at[2],
    )
    for copy in exchanges:
        copy.start()
    own_piece.start()

    panels = (lesser, advanced)
    started = []

    def panel_copy(matrix, dst, src, device):
        return remote(
            panels[matrix].at[src], panels[matrix].at[dst],
            send.at[matrix, dst], recv.at[matrix, dst], device,
        )

    def forward(matrix, dst, src, device):
        copy = panel_copy(matrix, dst, src, device)
        copy.start()
        started.append(copy)

    def arrived(matrix, slot):
        panel_copy(matrix, slot, slot, y_up).wait_recv()

    def to_neighbours(matrix):
        forward(matrix, 4, 0, y_up)
        forward(matrix, 2, 0, y_down)
        forward(matrix, 1, 0, x_pair)

    load_lesser.wait()
    to_neighbours(LESSER)

    def split(matrix, source, following):
        def step(t, carry):
            stage_copy(matrix, source, t).wait()
            value = stage[t % AHEAD]
            top = value.astype(BF16)
            rows = pl.ds(pl.multiple_of((t % 8) * 128, 128), 128)
            high[matrix, t // 8, rows, :] = top
            low[matrix, t // 8, rows, :] = (value - top.astype(F32)).astype(BF16)

            @pl.when(t + AHEAD < 16)
            def _():
                stage_copy(matrix, source, t + AHEAD).start()

            if following is not None:
                @pl.when(t + AHEAD >= 16)
                def _():
                    stage_copy(1, following, t + AHEAD - 16).start()
            return carry

        lax.fori_loop(0, 16, step, 0)

    split(0, sigma_ret, sigma_less)
    own_piece.wait()
    for copy in exchanges:
        copy.wait_recv()
    to_neighbours(ADVANCED)
    split(1, sigma_less, None)

    def chip_copy(slot, tile):
        rows = pl.ds(pl.multiple_of(tile * TILE, TILE), TILE)
        return remote(
            part.at[slot, 0, rows, :], part_in.at[slot, rows, :],
            chip_send.at[slot, tile], chip_recv.at[slot, tile], at_row(0, 0, 1),
        )

    def z_copy(slot, p):
        return remote(
            part.at[slot, 1, pl.ds(p * 256, 256), :], z_in.at[slot, p],
            z_send.at[slot, p], z_recv.at[slot, p], at_row(0, DZ[p], 0),
        )

    def x_copy(slot):
        return remote(
            x_out.at[slot], x_in.at[slot], x_send.at[slot], x_recv.at[slot], at_row(1, 0, 0)
        )

    def out_copy(slot):
        owner = at_col(slot % 2, DY[slot // 2])[0]
        return pltpu.make_async_copy(
            total.at[slot],
            out.at[:, pl.ds(pl.multiple_of(owner * 128, 128), 128)],
            out_sem.at[slot],
        )

    def product(slot):
        value = lesser[slot]
        top = value.astype(BF16)
        lesser_w[:, :128] = top
        lesser_w[:, 128:] = (value - top.astype(F32)).astype(BF16)
        value = advanced[slot]
        top = value.astype(BF16)
        advanced_w[:128, :] = top
        advanced_w[128:, :] = (value - top.astype(F32)).astype(BF16)

        def step(t, carry):
            half, tile = t // 2, t % 2
            rows = pl.ds(pl.multiple_of(tile * TILE, TILE), TILE)
            plain, turned = (((1,), (0,)), ((), ())), (((1,), (1,)), ((), ()))
            both = None
            for matrix, weights, dims in ((0, lesser_w, plain), (1, advanced_w, turned)):
                for piece in (high, low):
                    term = lax.dot_general(
                        piece[matrix, half, rows, :], weights[...], dims,
                        preferred_element_type=F32,
                    )
                    both = term if both is None else both + term
            part[slot, half, rows, :] = both[:, :128] + both[:, 128:]

            @pl.when(half == 0)
            def _():
                chip_copy(slot, tile).start()
            return carry

        lax.fori_loop(0, 4, step, 0)

    def chip_sum(slot):
        for tile in range(2):
            rows = pl.ds(tile * TILE, TILE)
            chip_copy(slot, tile).wait_recv()
            part[slot, 1, rows, :] += part_in[slot, rows, :]
            for p in (2 * tile, 2 * tile + 1):
                if p < 3:
                    z_copy(slot, p).start()

    def z_sum(slot):
        for p in range(3):
            z_copy(slot, p).wait_recv()
        own = part[slot, 1, 768:, :]
        summed = (own + z_in[slot, 0]) + (z_in[slot, 1] + z_in[slot, 2])
        total[slot] = summed[:128]
        x_out[slot] = summed[128:]
        x_copy(slot).start()

    def x_sum(slot):
        x_copy(slot).wait_recv()
        total[slot] += x_in[slot]
        out_copy(slot).start()

    for slot in range(8):
        if slot == 1:
            arrived(LESSER, 1)
            forward(LESSER, 5, 1, y_up)
            forward(LESSER, 3, 1, y_down)
            arrived(ADVANCED, 2)
            forward(ADVANCED, 3, 2, x_pair)
            arrived(LESSER, 4)
            forward(LESSER, 6, 4, y_up)
            forward(ADVANCED, 6, 2, y_down)
            arrived(ADVANCED, 4)
            forward(ADVANCED, 5, 4, x_pair)
            arrived(ADVANCED, 1)
        elif slot == 2:
            arrived(LESSER, 2)
        elif slot == 3:
            arrived(LESSER, 5)
            forward(LESSER, 7, 5, y_up)
            arrived(ADVANCED, 3)
            forward(ADVANCED, 7, 3, y_down)
            arrived(LESSER, 3)
        elif slot == 5:
            arrived(ADVANCED, 5)
        elif slot >= 6:
            arrived(LESSER, slot)
            arrived(ADVANCED, slot)
        product(slot)
        chip_sum(slot)
        if slot >= 2:
            z_sum(slot - 2)
        if slot >= 4:
            x_sum(slot - 4)
    for slot in (6, 7):
        z_sum(slot)
        x_sum(slot - 2)
    for slot in (6, 7):
        x_sum(slot)

    for copy in exchanges + started:
        copy.wait_send()
    for slot in range(8):
        for tile in range(2):
            chip_copy(slot, tile).wait_send()
        for p in range(3):
            z_copy(slot, p).wait_send()
        x_copy(slot).wait_send()
        out_copy(slot).wait()


def on_device(sigma_ret, sigma_less, green_less, green_ret):
    dma = pltpu.SemaphoreType.DMA
    return pl.pallas_call(
        kernel,
        out_shape=jax.ShapeDtypeStruct((128, 1024), F32),
        in_specs=[pl.BlockSpec(memory_space=pl.ANY)] * 4,
        out_specs=pl.BlockSpec(memory_space=pl.ANY),
        scratch_shapes=[
            pltpu.VMEM((8, 1024, 128), F32),
            pltpu.VMEM((8, 128, 1024), F32),
            pltpu.VMEM((8, 16384), F32),
            pltpu.VMEM((2, 2, 1024, 1024), BF16),
            pltpu.VMEM((2, 2, 1024, 1024), BF16),
            pltpu.VMEM((AHEAD, 128, 1024), F32),
            pltpu.VMEM((1024, 256), BF16),
            pltpu.VMEM((256, 1024), BF16),
            pltpu.VMEM((8, 2, 1024, 128), F32),
            pltpu.VMEM((8, 1024, 128), F32),
            pltpu.VMEM((8, 3, 256, 128), F32),
            pltpu.VMEM((8, 128, 128), F32),
            pltpu.VMEM((8, 128, 128), F32),
            pltpu.VMEM((8, 128, 128), F32),
            dma((3,)),
            dma((AHEAD,)),
            dma((ROWS - 1,)),
            dma((ROWS - 1,)),
            dma((2, 8)),
            dma((2, 8)),
            dma((8, 2)),
            dma((8, 2)),
            dma((8, 3)),
            dma((8, 3)),
            dma((8,)),
            dma((8,)),
            dma((8,)),
        ],
        compiler_params=pltpu.CompilerParams(
            collective_id=0, has_side_effects=True, vmem_limit_bytes=60 << 20
        ),
        name="collision",
    )(sigma_ret, sigma_less, green_less, green_ret)


def solution(mesh):
    placed = (P("col", "row"), P("col", "row"), P("row", "col"), P(("col", "row"), None))
    return jax.shard_map(
        on_device, mesh=mesh, in_specs=placed, out_specs=P(("col", "row"), None), check_vma=False
    )
```

```python
import jax
import jax.numpy as jnp
from jax import lax
from jax.experimental import pallas as pl
from jax.experimental.pallas import tpu as pltpu
from jax.sharding import PartitionSpec as P

MESH = pl.DeviceIdType.MESH
F32 = jnp.float32
BF16 = jnp.bfloat16

NY, NZ = 4, 4
COLS, ROWS = 8, 16

DY = (0, 1, 3, 2)
LESSER, ADVANCED = 0, 1
DZ = (2, 1, 3, 0)
TILE = 512
AHEAD = 8


def kernel(
    sigma_ret, sigma_less, green_less, green_ret, out,
    lesser, advanced, mirror, high, low, stage, lesser_w, advanced_w,
    part, part_in, z_in, x_out, x_in, total,
    load_sem, stage_sem, a2a_send, a2a_recv, send, recv,
    chip_send, chip_recv, z_send, z_recv, x_send, x_recv, far_in, far_send, far_recv, out_sem,
):
    col, row = lax.axis_index("col"), lax.axis_index("row")
    x_lo, y = col // NY, col % NY
    x_hi, z, core = row // (2 * NZ), (row // 2) % NZ, row % 2

    def at_col(dx, dy):
        return (((x_lo + dx) % 2) * NY + (y + dy) % NY, row)

    def at_row(dx, dz, dcore):
        return (col, ((x_hi + dx) % 2) * 2 * NZ + ((z + dz) % NZ) * 2 + (core + dcore) % 2)

    y_up, y_down, x_pair = at_col(0, 1), at_col(0, NY - 1), at_col(1, 0)

    load_lesser = pltpu.make_async_copy(green_less, lesser.at[0], load_sem.at[0])
    load_mirror = pltpu.make_async_copy(green_ret, mirror, load_sem.at[1])
    load_lesser.start()
    load_mirror.start()

    def stage_copy(matrix, source, t):
        half, p = t // 8, t % 8
        q = p // 2
        dz = jnp.where(q == 0, DZ[0], jnp.where(q == 1, DZ[1], jnp.where(q == 2, DZ[2], DZ[3])))
        block = at_row(p % 2, dz, 1 - half)[1]
        return pltpu.make_async_copy(
            source.at[pl.ds(pl.multiple_of(block * 128, 128), 128), :],
            stage.at[t % AHEAD],
            stage_sem.at[t % AHEAD],
        )

    for t in range(AHEAD):
        stage_copy(0, sigma_ret, t).start()

    barrier = pltpu.get_barrier_semaphore()
    peers = [y_up, y_down, x_pair] + [(col, (row + d) % ROWS) for d in range(1, ROWS)]
    for peer in peers:
        pl.semaphore_signal(barrier, inc=1, device_id=peer, device_id_type=MESH)
    pl.semaphore_wait(barrier, len(peers))

    def remote(src, dst, send_sem, recv_sem, device):
        return pltpu.make_async_remote_copy(
            src_ref=src, dst_ref=dst, send_sem=send_sem, recv_sem=recv_sem,
            device_id=device, device_id_type=MESH,
        )

    load_mirror.wait()
    exchanges = []
    mine = pl.ds(pl.multiple_of(row * 8, 8), 8)
    for d in range(1, ROWS):
        target = (row + d) % ROWS
        exchanges.append(remote(
            mirror.at[:, pl.ds(pl.multiple_of(target * 1024, 1024), 1024)],
            advanced.at[0, mine, :],
            a2a_send.at[d - 1], a2a_recv.at[d - 1], (col, target),
        ))
    own_piece = pltpu.make_async_copy(
        mirror.at[:, pl.ds(pl.multiple_of(row * 1024, 1024), 1024)],
        advanced.at[0, mine, :], load_sem.at[2],
    )
    for copy in exchanges:
        copy.start()
    own_piece.start()

    panels = (lesser, advanced)
    started = []

    def panel(matrix, slot, half):
        if half is None:
            return panels[matrix].at[slot]
        times = pl.ds(half * 512, 512)
        return lesser.at[slot, times, :] if matrix == LESSER else advanced.at[slot, :, times]

    def panel_copy(matrix, dst, src, device, half):
        index = (matrix, dst, half or 0)
        return remote(
            panel(matrix, src, half), panel(matrix, dst, half), send.at[index], recv.at[index], device
        )

    def forward(matrix, dst, src, device, half=None):
        copy = panel_copy(matrix, dst, src, device, half)
        copy.start()
        started.append(copy)

    def arrived(matrix, slot, half=None):
        panel_copy(matrix, slot, slot, y_up, half).wait_recv()

    def to_neighbours(matrix):
        forward(matrix, 4, 0, y_up)
        forward(matrix, 2, 0, y_down)
        forward(matrix, 1, 0, x_pair)

    load_lesser.wait()
    to_neighbours(LESSER)

    def split(matrix, source, following):
        def step(t, carry):
            stage_copy(matrix, source, t).wait()
            value = stage[t % AHEAD]
            top = value.astype(BF16)
            rest = (value - top.astype(F32)).astype(BF16)
            for group in range(2):
                rows = pl.ds(pl.multiple_of(group * 512 + (t % 8) * 64, 64), 64)
                high[matrix, t // 8, rows, :] = top[group * 64 : group * 64 + 64]
                low[matrix, t // 8, rows, :] = rest[group * 64 : group * 64 + 64]

            @pl.when(t + AHEAD < 16)
            def _():
                stage_copy(matrix, source, t + AHEAD).start()

            if following is not None:
                @pl.when(t + AHEAD >= 16)
                def _():
                    stage_copy(1, following, t + AHEAD - 16).start()
            return carry

        lax.fori_loop(0, 16, step, 0)

    def chip_copy(slot, tile):
        rows = pl.ds(pl.multiple_of(tile * TILE, TILE), TILE)
        return remote(
            part.at[slot, 0, rows, :], part_in.at[slot, rows, :],
            chip_send.at[slot, tile], chip_recv.at[slot, tile], at_row(0, 0, 1),
        )

    def z_copy(slot, p, group):
        return remote(
            part.at[slot, 1, pl.ds(group * 512 + p * 128, 128), :],
            z_in.at[slot, p, pl.ds(group * 128, 128), :],
            z_send.at[slot, 2 * p + group], z_recv.at[slot, 2 * p + group], at_row(0, DZ[p], 0),
        )

    def x_copy(slot):
        return remote(
            x_out.at[slot], x_in.at[slot], x_send.at[slot], x_recv.at[slot], at_row(1, 0, 0)
        )

    def out_copy(slot):
        owner = at_col(slot % 2, DY[slot // 2])[0]
        return pltpu.make_async_copy(
            total.at[slot],
            out.at[:, pl.ds(pl.multiple_of(owner * 128, 128), 128)],
            out_sem.at[slot],
        )

    def load_weights(slot, parts):
        for matrix, start, count in parts:
            times = pl.ds(start, count)
            if matrix == LESSER:
                value = lesser[slot, times, :]
                top = value.astype(BF16)
                lesser_w[times, :128] = top
                lesser_w[times, 128:] = (value - top.astype(F32)).astype(BF16)
            else:
                value = advanced[slot, :, times]
                top = value.astype(BF16)
                advanced_w[:128, times] = top
                advanced_w[128:, times] = (value - top.astype(F32)).astype(BF16)

    def tile_product(slot, parts, first, half, tile):
        rows = pl.ds(pl.multiple_of(tile * TILE, TILE), TILE)
        both = None
        for matrix, start, count in parts:
            times = pl.ds(start, count)
            if matrix == LESSER:
                weights, dims = lesser_w[times, :], (((1,), (0,)), ((), ()))
            else:
                weights, dims = advanced_w[:, times], (((1,), (1,)), ((), ()))
            for piece in (high, low):
                term = lax.dot_general(
                    piece[matrix, half, rows, times], weights, dims, preferred_element_type=F32
                )
                both = term if both is None else both + term
        both = both[:, :128] + both[:, 128:]
        if first:
            part[slot, half, rows, :] = both
        else:
            part[slot, half, rows, :] += both

    WHOLE = {LESSER: ((LESSER, 0, 1024),), ADVANCED: ((ADVANCED, 0, 1024),)}
    HALVES = [tuple((matrix, start, 512) for matrix in (LESSER, ADVANCED)) for start in (0, 512)]

    def begin(slot, parts):
        load_weights(slot, parts)

        def step(t, carry):
            tile_product(slot, parts, True, t // 2, t % 2)
            return carry

        lax.fori_loop(0, 4, step, 0)

    def finish(slot, parts, first=False):
        load_weights(slot, parts)

        def step(t, carry):
            half, tile = t // 2, t % 2
            tile_product(slot, parts, first, half, tile)

            @pl.when(half == 0)
            def _():
                chip_copy(slot, tile).start()
            return carry

        lax.fori_loop(0, 4, step, 0)
        for tile in range(2):
            chip_sum(slot, tile)
            depart(slot, tile)

    def chip_sum(slot, tile):
        rows = pl.ds(pl.multiple_of(tile * TILE, TILE), TILE)
        chip_copy(slot, tile).wait_recv()
        part[slot, 1, rows, :] += part_in[slot, rows, :]

    def z_total(slot, group):
        for p in range(3):
            z_copy(slot, p, group).wait_recv()
        own = part[slot, 1, group * 512 + 384 : group * 512 + 512, :]
        rows = pl.ds(group * 128, 128)
        return (own + z_in[slot, 0, rows, :]) + (z_in[slot, 1, rows, :] + z_in[slot, 2, rows, :])

    def z_sum(slot):
        for group in range(2):
            summed = z_total(slot, group)
            rows = pl.ds(group * 64, 64)
            total[slot, rows, :] = summed[:64]
            x_out[slot, rows, :] = summed[64:]
        x_copy(slot).start()

    def x_sum(slot):
        x_copy(slot).wait_recv()
        total[slot] += x_in[slot]
        out_copy(slot).start()

    MIXED = (6, 5, 7)

    def mixed_x(slot, p):
        n = MIXED.index(slot)
        return remote(
            part.at[slot, 1, pl.ds(p * 128 + 64, 64), :], far_in.at[n, p],
            far_send.at[n, p], far_recv.at[n, p], at_row(1, 0, 0),
        )

    def mixed_x_then_z(slot, p):
        return remote(
            part.at[slot, 1, pl.ds(p * 128, 64), :], z_in.at[slot, p, :64, :],
            z_send.at[slot, 2 * p], z_recv.at[slot, 2 * p], at_row(0, DZ[p], 0),
        )

    def mixed_z_then_x(slot):
        return remote(
            x_out.at[slot, :64, :], x_in.at[slot, :64, :],
            x_send.at[slot], x_recv.at[slot], at_row(1, 0, 0),
        )

    def depart(slot, group):
        if slot in MIXED and group == 0:
            for p in range(4):
                mixed_x(slot, p).start()
        else:
            for p in range(3):
                z_copy(slot, p, group).start()

    def mixed_sum(slot):
        n = MIXED.index(slot)
        for p in range(4):
            mixed_x(slot, p).wait_recv()
            part[slot, 1, p * 128 : p * 128 + 64, :] += far_in[n, p]
            if p < 3:
                mixed_x_then_z(slot, p).start()
        summed = z_total(slot, 1)
        x_out[slot, :64, :] = summed[64:]
        mixed_z_then_x(slot).start()
        total[slot, 64:, :] = summed[:64]

    def mixed_end(slot):
        mixed_z_then_x(slot).wait_recv()
        total[slot, 64:, :] += x_in[slot, :64, :]
        for p in range(3):
            mixed_x_then_z(slot, p).wait_recv()
        own = part[slot, 1, 384:448, :]
        total[slot, :64, :] = (own + z_in[slot, 0, :64, :]) + (
            z_in[slot, 1, :64, :] + z_in[slot, 2, :64, :]
        )
        out_copy(slot).start()

    def finish_last(slot, parts):
        load_weights(slot, parts)

        def leave(tile, carry):
            tile_product(slot, parts, False, 0, tile)
            chip_copy(slot, tile).start()
            return carry

        def keep(tile, carry):
            tile_product(slot, parts, False, 1, tile)
            chip_sum(slot, tile)
            for group in range(2):
                @pl.when(tile == group)
                def _():
                    depart(slot, group)
            return carry

        lax.fori_loop(0, 2, leave, 0)
        lax.fori_loop(0, 2, keep, 0)

    split(0, sigma_ret, sigma_less)
    begin(0, WHOLE[LESSER])
    split(1, sigma_less, None)
    own_piece.wait()
    for copy in exchanges:
        copy.wait_recv()
    to_neighbours(ADVANCED)
    finish(0, WHOLE[ADVANCED])
    arrived(LESSER, 2)
    begin(2, WHOLE[LESSER])
    arrived(LESSER, 4)
    begin(4, WHOLE[LESSER])
    arrived(LESSER, 1)
    forward(LESSER, 5, 1, y_up)
    forward(LESSER, 3, 1, y_down)
    forward(LESSER, 6, 4, y_up)
    begin(1, WHOLE[LESSER])
    arrived(ADVANCED, 2)
    forward(ADVANCED, 3, 2, x_pair, 0)
    forward(ADVANCED, 3, 2, x_pair, 1)
    forward(ADVANCED, 6, 2, y_down)
    z_sum(0)
    arrived(ADVANCED, 4)
    forward(ADVANCED, 5, 4, x_pair)
    finish(2, WHOLE[ADVANCED])
    finish(4, WHOLE[ADVANCED])
    arrived(ADVANCED, 1)
    finish(1, WHOLE[ADVANCED])
    arrived(LESSER, 5)
    forward(LESSER, 7, 5, y_up, 0)
    forward(LESSER, 7, 5, y_up, 1)
    begin(5, WHOLE[LESSER])
    arrived(ADVANCED, 3, 0)
    forward(ADVANCED, 7, 3, y_down, 0)
    arrived(LESSER, 3)
    begin(3, WHOLE[LESSER])
    z_sum(2)
    arrived(ADVANCED, 3, 1)
    forward(ADVANCED, 7, 3, y_down, 1)
    finish(3, WHOLE[ADVANCED])
    z_sum(4)
    arrived(LESSER, 6)
    arrived(ADVANCED, 6)
    finish(6, WHOLE[LESSER] + WHOLE[ADVANCED], True)
    z_sum(1)
    arrived(LESSER, 7, 0)
    arrived(ADVANCED, 7, 0)
    begin(7, HALVES[0])
    arrived(ADVANCED, 5)
    finish(5, WHOLE[ADVANCED])
    z_sum(3)
    mixed_sum(6)
    arrived(LESSER, 7, 1)
    arrived(ADVANCED, 7, 1)
    finish_last(7, HALVES[1])
    x_sum(0)
    x_sum(2)
    x_sum(4)
    x_sum(1)
    mixed_sum(5)
    x_sum(3)
    mixed_sum(7)
    mixed_end(6)
    mixed_end(5)
    mixed_end(7)

    for copy in exchanges + started:
        copy.wait_send()
    for slot in range(8):
        for tile in range(2):
            chip_copy(slot, tile).wait_send()
        out_copy(slot).wait()
        for p in range(3):
            z_copy(slot, p, 1).wait_send()
        if slot in MIXED:
            for p in range(4):
                mixed_x(slot, p).wait_send()
            for p in range(3):
                mixed_x_then_z(slot, p).wait_send()
            mixed_z_then_x(slot).wait_send()
        else:
            for p in range(3):
                z_copy(slot, p, 0).wait_send()
            x_copy(slot).wait_send()


def on_device(sigma_ret, sigma_less, green_less, green_ret):
    dma = pltpu.SemaphoreType.DMA
    return pl.pallas_call(
        kernel,
        out_shape=jax.ShapeDtypeStruct((128, 1024), F32),
        in_specs=[pl.BlockSpec(memory_space=pltpu.HBM)] * 4,
        out_specs=pl.BlockSpec(memory_space=pl.ANY),
        scratch_shapes=[
            pltpu.VMEM((8, 1024, 128), F32),
            pltpu.VMEM((8, 128, 1024), F32),
            pltpu.VMEM((8, 16384), F32),
            pltpu.VMEM((2, 2, 1024, 1024), BF16),
            pltpu.VMEM((2, 2, 1024, 1024), BF16),
            pltpu.VMEM((AHEAD, 128, 1024), F32),
            pltpu.VMEM((1024, 256), BF16),
            pltpu.VMEM((256, 1024), BF16),
            pltpu.VMEM((8, 2, 1024, 128), F32),
            pltpu.VMEM((8, 1024, 128), F32),
            pltpu.VMEM((8, 3, 256, 128), F32),
            pltpu.VMEM((8, 128, 128), F32),
            pltpu.VMEM((8, 128, 128), F32),
            pltpu.VMEM((8, 128, 128), F32),
            dma((3,)),
            dma((AHEAD,)),
            dma((ROWS - 1,)),
            dma((ROWS - 1,)),
            dma((2, 8, 2)),
            dma((2, 8, 2)),
            dma((8, 2)),
            dma((8, 2)),
            dma((8, 6)),
            dma((8, 6)),
            dma((8,)),
            dma((8,)),
            pltpu.VMEM((3, 4, 64, 128), F32),
            dma((3, 4)),
            dma((3, 4)),
            dma((8,)),
        ],
        compiler_params=pltpu.CompilerParams(
            collective_id=0, has_side_effects=True, vmem_limit_bytes=53 << 20
        ),
        name="collision",
    )(sigma_ret, sigma_less, green_less, green_ret)


def solution(mesh):
    placed = (P("col", "row"), P("col", "row"), P("row", "col"), P(("col", "row"), None))
    return jax.shard_map(
        on_device, mesh=mesh, in_specs=placed, out_specs=P(("col", "row"), None), check_vma=False
    )
```

```python
import jax
import jax.numpy as jnp
from jax import lax
from jax.experimental import pallas as pl
from jax.experimental.pallas import tpu as pltpu
from jax.sharding import PartitionSpec as P

MESH = pl.DeviceIdType.MESH
F32 = jnp.float32
BF16 = jnp.bfloat16

NY, NZ = 4, 4
COLS, ROWS = 8, 16

DY = (0, 1, 3, 2)
LESSER, ADVANCED = 0, 1
DZ = (2, 1, 3, 0)
TILE = 512
AHEAD = 8


def kernel(
    sigma_ret, sigma_less, green_less, green_ret, out,
    lesser, advanced, mirror, high, low, stage, lesser_w, advanced_w,
    part, part_in, z_in, x_out, x_in, total,
    load_sem, stage_sem, a2a_send, a2a_recv, send, recv,
    chip_send, chip_recv, z_send, z_recv, x_send, x_recv, far_in, far_send, far_recv, out_sem, ready_sem,
):
    col, row = lax.axis_index("col"), lax.axis_index("row")
    x_lo, y = col // NY, col % NY
    x_hi, z, core = row // (2 * NZ), (row // 2) % NZ, row % 2

    def at_col(dx, dy):
        return (((x_lo + dx) % 2) * NY + (y + dy) % NY, row)

    def at_row(dx, dz, dcore):
        return (col, ((x_hi + dx) % 2) * 2 * NZ + ((z + dz) % NZ) * 2 + (core + dcore) % 2)

    y_up, y_down, x_pair = at_col(0, 1), at_col(0, NY - 1), at_col(1, 0)

    load_lesser = pltpu.make_async_copy(green_less, lesser.at[0], load_sem.at[0])
    load_mirror = pltpu.make_async_copy(green_ret, mirror, load_sem.at[1])
    load_lesser.start()
    load_mirror.start()

    def stage_copy(matrix, source, t):
        half, p = t // 8, t % 8
        q = p // 2
        dz = jnp.where(q == 0, DZ[0], jnp.where(q == 1, DZ[1], jnp.where(q == 2, DZ[2], DZ[3])))
        block = at_row(p % 2, dz, 1 - half)[1]
        return pltpu.make_async_copy(
            source.at[pl.ds(pl.multiple_of(block * 128, 128), 128), :],
            stage.at[t % AHEAD],
            stage_sem.at[t % AHEAD],
        )

    for t in range(AHEAD):
        stage_copy(0, sigma_ret, t).start()

    def meet(semaphore, peers):
        for peer in peers:
            pl.semaphore_signal(semaphore, inc=1, device_id=peer, device_id_type=MESH)
        pl.semaphore_wait(semaphore, len(peers))

    z_mates = [at_row(0, d, 0) for d in range(1, NZ)]
    chip_mate = at_row(0, 0, 1)
    meet(
        pltpu.get_barrier_semaphore(),
        [y_up, y_down, x_pair, chip_mate, at_row(1, 0, 0)] + z_mates,
    )

    def remote(src, dst, send_sem, recv_sem, device):
        return pltpu.make_async_remote_copy(
            src_ref=src, dst_ref=dst, send_sem=send_sem, recv_sem=recv_sem,
            device_id=device, device_id_type=MESH,
        )

    panels = (lesser, advanced)
    started = []

    def panel(matrix, slot, half):
        if half is None:
            return panels[matrix].at[slot]
        times = pl.ds(half * 512, 512)
        return lesser.at[slot, times, :] if matrix == LESSER else advanced.at[slot, :, times]

    def panel_copy(matrix, dst, src, device, half):
        index = (matrix, dst, half or 0)
        return remote(
            panel(matrix, src, half), panel(matrix, dst, half), send.at[index], recv.at[index], device
        )

    def forward(matrix, dst, src, device, half=None):
        copy = panel_copy(matrix, dst, src, device, half)
        copy.start()
        started.append(copy)

    def arrived(matrix, slot, half=None):
        panel_copy(matrix, slot, slot, y_up, half).wait_recv()

    load_lesser.wait()
    forward(LESSER, 4, 0, y_up)
    forward(LESSER, 2, 0, y_down)

    meet(ready_sem.at[0], z_mates)
    meet(ready_sem.at[1], [chip_mate])

    load_mirror.wait()
    exchanges = []
    mine = pl.ds(pl.multiple_of(row * 8, 8), 8)
    for d in range(1, ROWS):
        target = (row + d) % ROWS
        exchanges.append(remote(
            mirror.at[:, pl.ds(pl.multiple_of(target * 1024, 1024), 1024)],
            advanced.at[0, mine, :],
            a2a_send.at[d - 1], a2a_recv.at[d - 1], (col, target),
        ))
    own_piece = pltpu.make_async_copy(
        mirror.at[:, pl.ds(pl.multiple_of(row * 1024, 1024), 1024)],
        advanced.at[0, mine, :], load_sem.at[2],
    )
    for copy in exchanges:
        copy.start()
    own_piece.start()
    forward(LESSER, 1, 0, x_pair)


    def split(matrix, source, following):
        def step(t, carry):
            stage_copy(matrix, source, t).wait()
            value = stage[t % AHEAD]
            top = value.astype(BF16)
            rest = (value - top.astype(F32)).astype(BF16)
            for group in range(2):
                rows = pl.ds(pl.multiple_of(group * 512 + (t % 8) * 64, 64), 64)
                high[matrix, t // 8, rows, :] = top[group * 64 : group * 64 + 64]
                low[matrix, t // 8, rows, :] = rest[group * 64 : group * 64 + 64]

            @pl.when(t + AHEAD < 16)
            def _():
                stage_copy(matrix, source, t + AHEAD).start()

            if following is not None:
                @pl.when(t + AHEAD >= 16)
                def _():
                    stage_copy(1, following, t + AHEAD - 16).start()
            return carry

        lax.fori_loop(0, 16, step, 0)

    def chip_copy(slot, tile):
        rows = pl.ds(pl.multiple_of(tile * TILE, TILE), TILE)
        return remote(
            part.at[slot, 0, rows, :], part_in.at[slot, rows, :],
            chip_send.at[slot, tile], chip_recv.at[slot, tile], at_row(0, 0, 1),
        )

    def z_copy(slot, p, group):
        return remote(
            part.at[slot, 1, pl.ds(group * 512 + p * 128, 128), :],
            z_in.at[slot, p, pl.ds(group * 128, 128), :],
            z_send.at[slot, 2 * p + group], z_recv.at[slot, 2 * p + group], at_row(0, DZ[p], 0),
        )

    def x_copy(slot):
        return remote(
            x_out.at[slot], x_in.at[slot], x_send.at[slot], x_recv.at[slot], at_row(1, 0, 0)
        )

    def out_copy(slot):
        owner = at_col(slot % 2, DY[slot // 2])[0]
        return pltpu.make_async_copy(
            total.at[slot],
            out.at[:, pl.ds(pl.multiple_of(owner * 128, 128), 128)],
            out_sem.at[slot],
        )

    def load_weights(slot, parts):
        for matrix, start, count in parts:
            times = pl.ds(start, count)
            if matrix == LESSER:
                value = lesser[slot, times, :]
                top = value.astype(BF16)
                lesser_w[times, :128] = top
                lesser_w[times, 128:] = (value - top.astype(F32)).astype(BF16)
            else:
                value = advanced[slot, :, times]
                top = value.astype(BF16)
                advanced_w[:128, times] = top
                advanced_w[128:, times] = (value - top.astype(F32)).astype(BF16)

    def tile_product(slot, parts, first, half, tile, height=TILE):
        rows = pl.ds(pl.multiple_of(tile * height, height), height)
        both = None
        for matrix, start, count in parts:
            times = pl.ds(start, count)
            if matrix == LESSER:
                weights, dims = lesser_w[times, :], (((1,), (0,)), ((), ()))
            else:
                weights, dims = advanced_w[:, times], (((1,), (1,)), ((), ()))
            for piece in (high, low):
                term = lax.dot_general(
                    piece[matrix, half, rows, times], weights, dims, preferred_element_type=F32
                )
                both = term if both is None else both + term
        both = both[:, :128] + both[:, 128:]
        if first:
            part[slot, half, rows, :] = both
        else:
            part[slot, half, rows, :] += both

    WHOLE = {LESSER: ((LESSER, 0, 1024),), ADVANCED: ((ADVANCED, 0, 1024),)}
    HALVES = [tuple((matrix, start, 512) for matrix in (LESSER, ADVANCED)) for start in (0, 512)]

    def begin(slot, parts):
        load_weights(slot, parts)

        def step(half, carry):
            tile_product(slot, parts, True, half, 0, 2 * TILE)
            return carry

        lax.fori_loop(0, 2, step, 0)

    def finish(slot, parts):
        load_weights(slot, parts)

        def step(tile, carry):
            tile_product(slot, parts, False, 0, tile)
            chip_copy(slot, tile).start()
            return carry

        lax.fori_loop(0, 2, step, 0)
        tile_product(slot, parts, False, 1, 0, 2 * TILE)
        for tile in range(2):
            chip_sum(slot, tile)
            depart(slot, tile)

    def chip_sum(slot, tile):
        rows = pl.ds(pl.multiple_of(tile * TILE, TILE), TILE)
        chip_copy(slot, tile).wait_recv()
        part[slot, 1, rows, :] += part_in[slot, rows, :]

    def z_total(slot, group):
        for p in range(3):
            z_copy(slot, p, group).wait_recv()
        own = part[slot, 1, group * 512 + 384 : group * 512 + 512, :]
        rows = pl.ds(group * 128, 128)
        return (own + z_in[slot, 0, rows, :]) + (z_in[slot, 1, rows, :] + z_in[slot, 2, rows, :])

    def z_sum(slot):
        for group in range(2):
            summed = z_total(slot, group)
            rows = pl.ds(group * 64, 64)
            total[slot, rows, :] = summed[:64]
            x_out[slot, rows, :] = summed[64:]
        x_copy(slot).start()

    def x_sum(slot):
        x_copy(slot).wait_recv()
        total[slot] += x_in[slot]
        out_copy(slot).start()

    MIXED = (5, 7)

    def mixed_x(slot, p):
        n = MIXED.index(slot)
        return remote(
            part.at[slot, 1, pl.ds(p * 128 + 64, 64), :], far_in.at[n, p],
            far_send.at[n, p], far_recv.at[n, p], at_row(1, 0, 0),
        )

    def mixed_x_then_z(slot, p):
        return remote(
            part.at[slot, 1, pl.ds(p * 128, 64), :], z_in.at[slot, p, :64, :],
            z_send.at[slot, 2 * p], z_recv.at[slot, 2 * p], at_row(0, DZ[p], 0),
        )

    def mixed_z_then_x(slot):
        return remote(
            x_out.at[slot, :64, :], x_in.at[slot, :64, :],
            x_send.at[slot], x_recv.at[slot], at_row(1, 0, 0),
        )

    def depart(slot, group):
        if slot in MIXED and group == 0:
            for p in range(4):
                mixed_x(slot, p).start()
        else:
            for p in range(3):
                z_copy(slot, p, group).start()

    def mixed_sum(slot):
        n = MIXED.index(slot)
        for p in range(4):
            mixed_x(slot, p).wait_recv()
            part[slot, 1, p * 128 : p * 128 + 64, :] += far_in[n, p]
            if p < 3:
                mixed_x_then_z(slot, p).start()
        summed = z_total(slot, 1)
        x_out[slot, :64, :] = summed[64:]
        mixed_z_then_x(slot).start()
        total[slot, 64:, :] = summed[:64]

    def mixed_end(slot):
        mixed_z_then_x(slot).wait_recv()
        total[slot, 64:, :] += x_in[slot, :64, :]
        for p in range(3):
            mixed_x_then_z(slot, p).wait_recv()
        own = part[slot, 1, 384:448, :]
        total[slot, :64, :] = (own + z_in[slot, 0, :64, :]) + (
            z_in[slot, 1, :64, :] + z_in[slot, 2, :64, :]
        )
        out_copy(slot).start()

    def finish_last(slot, parts):
        load_weights(slot, parts)

        def leave(tile, carry):
            tile_product(slot, parts, False, 0, tile)
            chip_copy(slot, tile).start()
            return carry

        def keep(tile, carry):
            tile_product(slot, parts, False, 1, tile)
            chip_sum(slot, tile)
            for group in range(2):
                @pl.when(tile == group)
                def _():
                    depart(slot, group)
            return carry

        lax.fori_loop(0, 2, leave, 0)
        lax.fori_loop(0, 2, keep, 0)

    split(0, sigma_ret, sigma_less)
    begin(0, WHOLE[LESSER])
    split(1, sigma_less, None)
    own_piece.wait()
    for copy in exchanges:
        copy.wait_recv()
    forward(ADVANCED, 4, 0, y_up)
    forward(ADVANCED, 2, 0, y_down)
    forward(ADVANCED, 1, 0, x_pair)
    finish(0, WHOLE[ADVANCED])
    arrived(LESSER, 2)
    begin(2, WHOLE[LESSER])
    arrived(LESSER, 4)
    begin(4, WHOLE[LESSER])
    arrived(LESSER, 1)
    forward(LESSER, 5, 1, y_up)
    forward(LESSER, 3, 1, y_down)
    forward(LESSER, 6, 4, y_up, 0)
    forward(LESSER, 6, 4, y_up, 1)
    begin(1, WHOLE[LESSER])
    arrived(ADVANCED, 2)
    forward(ADVANCED, 3, 2, x_pair, 0)
    forward(ADVANCED, 3, 2, x_pair, 1)
    forward(ADVANCED, 6, 2, y_down, 0)
    forward(ADVANCED, 6, 2, y_down, 1)
    z_sum(0)
    arrived(ADVANCED, 4)
    forward(ADVANCED, 5, 4, x_pair)
    finish(2, WHOLE[ADVANCED])
    finish(4, WHOLE[ADVANCED])
    arrived(ADVANCED, 1)
    finish(1, WHOLE[ADVANCED])
    arrived(LESSER, 5)
    forward(LESSER, 7, 5, y_up, 0)
    forward(LESSER, 7, 5, y_up, 1)
    begin(5, WHOLE[LESSER])
    arrived(ADVANCED, 3, 0)
    forward(ADVANCED, 7, 3, y_down, 0)
    arrived(LESSER, 3)
    begin(3, WHOLE[LESSER])
    z_sum(2)
    arrived(ADVANCED, 3, 1)
    forward(ADVANCED, 7, 3, y_down, 1)
    finish(3, WHOLE[ADVANCED])
    z_sum(4)
    arrived(LESSER, 6, 0)
    arrived(ADVANCED, 6, 0)
    begin(6, HALVES[0])
    z_sum(1)
    arrived(LESSER, 6, 1)
    arrived(ADVANCED, 6, 1)
    finish(6, HALVES[1])
    arrived(LESSER, 7, 0)
    arrived(ADVANCED, 7, 0)
    begin(7, HALVES[0])
    arrived(ADVANCED, 5)
    finish(5, WHOLE[ADVANCED])
    z_sum(3)
    arrived(LESSER, 7, 1)
    arrived(ADVANCED, 7, 1)
    finish_last(7, HALVES[1])
    z_sum(6)
    x_sum(0)
    x_sum(2)
    x_sum(4)
    x_sum(1)
    mixed_sum(5)
    x_sum(3)
    mixed_sum(7)
    x_sum(6)
    mixed_end(5)
    mixed_end(7)

    for copy in exchanges + started:
        copy.wait_send()
    for slot in range(8):
        for tile in range(2):
            chip_copy(slot, tile).wait_send()
        out_copy(slot).wait()
        for p in range(3):
            z_copy(slot, p, 1).wait_send()
        if slot in MIXED:
            for p in range(4):
                mixed_x(slot, p).wait_send()
            for p in range(3):
                mixed_x_then_z(slot, p).wait_send()
            mixed_z_then_x(slot).wait_send()
        else:
            for p in range(3):
                z_copy(slot, p, 0).wait_send()
            x_copy(slot).wait_send()


def on_device(sigma_ret, sigma_less, green_less, green_ret):
    dma = pltpu.SemaphoreType.DMA
    return pl.pallas_call(
        kernel,
        out_shape=jax.ShapeDtypeStruct((128, 1024), F32),
        in_specs=[pl.BlockSpec(memory_space=pltpu.HBM)] * 4,
        out_specs=pl.BlockSpec(memory_space=pl.ANY),
        scratch_shapes=[
            pltpu.VMEM((8, 1024, 128), F32),
            pltpu.VMEM((8, 128, 1024), F32),
            pltpu.VMEM((8, 16384), F32),
            pltpu.VMEM((2, 2, 1024, 1024), BF16),
            pltpu.VMEM((2, 2, 1024, 1024), BF16),
            pltpu.VMEM((AHEAD, 128, 1024), F32),
            pltpu.VMEM((1024, 256), BF16),
            pltpu.VMEM((256, 1024), BF16),
            pltpu.VMEM((8, 2, 1024, 128), F32),
            pltpu.VMEM((8, 1024, 128), F32),
            pltpu.VMEM((8, 3, 256, 128), F32),
            pltpu.VMEM((8, 128, 128), F32),
            pltpu.VMEM((8, 128, 128), F32),
            pltpu.VMEM((8, 128, 128), F32),
            dma((3,)),
            dma((AHEAD,)),
            dma((ROWS - 1,)),
            dma((ROWS - 1,)),
            dma((2, 8, 2)),
            dma((2, 8, 2)),
            dma((8, 2)),
            dma((8, 2)),
            dma((8, 6)),
            dma((8, 6)),
            dma((8,)),
            dma((8,)),
            pltpu.VMEM((2, 4, 64, 128), F32),
            dma((2, 4)),
            dma((2, 4)),
            dma((8,)),
            pltpu.SemaphoreType.REGULAR((2,)),
        ],
        compiler_params=pltpu.CompilerParams(
            collective_id=0, has_side_effects=True, vmem_limit_bytes=53 << 20
        ),
        name="collision",
    )(sigma_ret, sigma_less, green_less, green_ret)


def solution(mesh):
    placed = (P("col", "row"), P("col", "row"), P("row", "col"), P(("col", "row"), None))
    return jax.shard_map(
        on_device, mesh=mesh, in_specs=placed, out_specs=P(("col", "row"), None), check_vma=False
    )
```

```python
import jax
import jax.numpy as jnp
from jax import lax
from jax.experimental import pallas as pl
from jax.experimental.pallas import tpu as pltpu
from jax.sharding import PartitionSpec as P

MESH = pl.DeviceIdType.MESH
F32 = jnp.float32
BF16 = jnp.bfloat16

NY, NZ = 4, 4
COLS, ROWS = 8, 16

DY = (0, 1, 3, 2)
LESSER, ADVANCED = 0, 1
DZ = (2, 1, 3, 0)
TILE = 512
AHEAD = 8


def kernel(
    sigma_ret, sigma_less, green_less, green_ret, out,
    lesser, advanced, mirror, high, low, stage, lesser_w, advanced_w,
    part, part_in, z_in, x_out, x_in, total,
    load_sem, stage_sem, a2a_send, a2a_recv, send, recv,
    chip_send, chip_recv, z_send, z_recv, x_send, x_recv, far_in, far_send, far_recv, out_sem, ready_sem,
):
    col, row = lax.axis_index("col"), lax.axis_index("row")
    x_lo, y = col // NY, col % NY
    x_hi, z, core = row // (2 * NZ), (row // 2) % NZ, row % 2

    def at_col(dx, dy):
        return (((x_lo + dx) % 2) * NY + (y + dy) % NY, row)

    def at_row(dx, dz, dcore):
        return (col, ((x_hi + dx) % 2) * 2 * NZ + ((z + dz) % NZ) * 2 + (core + dcore) % 2)

    y_up, y_down, x_pair = at_col(0, 1), at_col(0, NY - 1), at_col(1, 0)

    load_lesser = pltpu.make_async_copy(green_less, lesser.at[0], load_sem.at[0])
    load_mirror = pltpu.make_async_copy(green_ret, mirror, load_sem.at[1])
    load_lesser.start()
    load_mirror.start()

    def stage_copy(matrix, source, t):
        half, p = t // 8, t % 8
        q = p // 2
        dz = jnp.where(q == 0, DZ[0], jnp.where(q == 1, DZ[1], jnp.where(q == 2, DZ[2], DZ[3])))
        block = at_row(p % 2, dz, 1 - half)[1]
        return pltpu.make_async_copy(
            source.at[pl.ds(pl.multiple_of(block * 128, 128), 128), :],
            stage.at[t % AHEAD],
            stage_sem.at[t % AHEAD],
        )

    for t in range(AHEAD):
        stage_copy(0, sigma_ret, t).start()

    def meet(semaphore, peers):
        for peer in peers:
            pl.semaphore_signal(semaphore, inc=1, device_id=peer, device_id_type=MESH)
        pl.semaphore_wait(semaphore, len(peers))

    z_mates = [at_row(0, d, 0) for d in range(1, NZ)]
    chip_mate = at_row(0, 0, 1)
    meet(
        pltpu.get_barrier_semaphore(),
        [y_up, y_down, x_pair, chip_mate, at_row(1, 0, 0)] + z_mates,
    )

    def remote(src, dst, send_sem, recv_sem, device):
        return pltpu.make_async_remote_copy(
            src_ref=src, dst_ref=dst, send_sem=send_sem, recv_sem=recv_sem,
            device_id=device, device_id_type=MESH,
        )

    panels = (lesser, advanced)

    def panel(matrix, slot, half):
        if half is None:
            return panels[matrix].at[slot]
        times = pl.ds(half * 512, 512)
        return lesser.at[slot, times, :] if matrix == LESSER else advanced.at[slot, :, times]

    def panel_copy(matrix, dst, src, device, half):
        index = (matrix, dst, half or 0)
        return remote(
            panel(matrix, src, half), panel(matrix, dst, half), send, recv.at[index], device
        )

    def forward(matrix, dst, src, device, half=None):
        copy = panel_copy(matrix, dst, src, device, half)
        copy.start()

    def arrived(matrix, slot, half=None):
        panel_copy(matrix, slot, slot, y_up, half).wait_recv()

    load_lesser.wait()
    forward(LESSER, 4, 0, y_up)
    forward(LESSER, 2, 0, y_down)

    meet(ready_sem.at[0], z_mates)
    meet(ready_sem.at[1], [chip_mate])

    def wait_bytes(semaphore, ref):
        pltpu.make_async_copy(ref, ref, semaphore).wait()

    load_mirror.wait()
    exchanges = []
    mine = pl.ds(pl.multiple_of(row * 8, 8), 8)
    for d in range(1, ROWS):
        target = (row + d) % ROWS
        exchanges.append(remote(
            mirror.at[:, pl.ds(pl.multiple_of(target * 1024, 1024), 1024)],
            advanced.at[0, mine, :],
            a2a_send, a2a_recv, (col, target),
        ))
    own_piece = pltpu.make_async_copy(
        mirror.at[:, pl.ds(pl.multiple_of(row * 1024, 1024), 1024)],
        advanced.at[0, mine, :], load_sem.at[2],
    )
    for copy in exchanges:
        copy.start()
    own_piece.start()
    forward(LESSER, 1, 0, x_pair)


    def split(matrix, source, following):
        def step(t, carry):
            stage_copy(matrix, source, t).wait()
            value = stage[t % AHEAD]
            top = value.astype(BF16)
            rest = (value - top.astype(F32)).astype(BF16)
            for group in range(2):
                rows = pl.ds(pl.multiple_of(group * 512 + (t % 8) * 64, 64), 64)
                high[matrix, t // 8, rows, :] = top[group * 64 : group * 64 + 64]
                low[matrix, t // 8, rows, :] = rest[group * 64 : group * 64 + 64]

            @pl.when(t + AHEAD < 16)
            def _():
                stage_copy(matrix, source, t + AHEAD).start()

            if following is not None:
                @pl.when(t + AHEAD >= 16)
                def _():
                    stage_copy(1, following, t + AHEAD - 16).start()
            return carry

        lax.fori_loop(0, 16, step, 0)

    MIXED = (5, 7)

    def chip_copy(slot, tile):
        rows = pl.ds(pl.multiple_of(tile * TILE, TILE), TILE)
        return remote(
            part.at[slot, 0, rows, :], part_in.at[slot, rows, :],
            chip_send, chip_recv.at[slot, tile], at_row(0, 0, 1),
        )

    def z_copy(slot, p, group):
        return remote(
            part.at[slot, 1, pl.ds(group * 512 + p * 128, 128), :],
            z_in.at[slot, p, pl.ds(group * 128, 128), :],
            z_send.at[MIXED.index(slot) + 1 if slot in MIXED else 0], z_recv.at[slot, group],
            at_row(0, DZ[p], 0),
        )

    def x_copy(slot):
        return remote(
            x_out.at[slot], x_in.at[slot], x_send.at[0], x_recv.at[slot], at_row(1, 0, 0)
        )

    def out_copy(slot):
        owner = at_col(slot % 2, DY[slot // 2])[0]
        return pltpu.make_async_copy(
            total.at[slot],
            out.at[:, pl.ds(pl.multiple_of(owner * 128, 128), 128)],
            out_sem,
        )

    def load_weights(slot, parts):
        for matrix, start, count in parts:
            times = pl.ds(start, count)
            if matrix == LESSER:
                value = lesser[slot, times, :]
                top = value.astype(BF16)
                lesser_w[times, :128] = top
                lesser_w[times, 128:] = (value - top.astype(F32)).astype(BF16)
            else:
                value = advanced[slot, :, times]
                top = value.astype(BF16)
                advanced_w[:128, times] = top
                advanced_w[128:, times] = (value - top.astype(F32)).astype(BF16)

    def tile_product(slot, parts, first, half, tile, height=TILE):
        rows = pl.ds(pl.multiple_of(tile * height, height), height)
        both = None
        for matrix, start, count in parts:
            times = pl.ds(start, count)
            if matrix == LESSER:
                weights, dims = lesser_w[times, :], (((1,), (0,)), ((), ()))
            else:
                weights, dims = advanced_w[:, times], (((1,), (1,)), ((), ()))
            for piece in (high, low):
                term = lax.dot_general(
                    piece[matrix, half, rows, times], weights, dims, preferred_element_type=F32
                )
                both = term if both is None else both + term
        both = both[:, :128] + both[:, 128:]
        if first:
            part[slot, half, rows, :] = both
        else:
            part[slot, half, rows, :] += both

    WHOLE = {LESSER: ((LESSER, 0, 1024),), ADVANCED: ((ADVANCED, 0, 1024),)}
    HALVES = [tuple((matrix, start, 512) for matrix in (LESSER, ADVANCED)) for start in (0, 512)]

    def begin(slot, parts, first=True):
        load_weights(slot, parts)

        def step(half, carry):
            tile_product(slot, parts, first, half, 0, 2 * TILE)
            return carry

        lax.fori_loop(0, 2, step, 0)

    def finish(slot, parts):
        load_weights(slot, parts)

        def step(tile, carry):
            tile_product(slot, parts, False, 0, tile)
            chip_copy(slot, tile).start()
            return carry

        lax.fori_loop(0, 2, step, 0)
        tile_product(slot, parts, False, 1, 0, 2 * TILE)
        for tile in range(2):
            chip_sum(slot, tile)
            depart(slot, tile)

    def chip_sum(slot, tile):
        rows = pl.ds(pl.multiple_of(tile * TILE, TILE), TILE)
        chip_copy(slot, tile).wait_recv()
        part[slot, 1, rows, :] += part_in[slot, rows, :]

    def z_total(slot, group):
        wait_bytes(z_recv.at[slot, group], z_in.at[slot, :, pl.ds(group * 128, 128), :])
        own = part[slot, 1, group * 512 + 384 : group * 512 + 512, :]
        rows = pl.ds(group * 128, 128)
        return (own + z_in[slot, 0, rows, :]) + (z_in[slot, 1, rows, :] + z_in[slot, 2, rows, :])

    def z_sum(slot):
        for group in range(2):
            summed = z_total(slot, group)
            rows = pl.ds(group * 64, 64)
            total[slot, rows, :] = summed[:64]
            x_out[slot, rows, :] = summed[64:]
        x_copy(slot).start()

    def x_sum(slot):
        x_copy(slot).wait_recv()
        total[slot] += x_in[slot]
        out_copy(slot).start()


    def mixed_x(slot, p):
        n = MIXED.index(slot)
        return remote(
            part.at[slot, 1, pl.ds(p * 128 + 64, 64), :], far_in.at[n, p],
            far_send, far_recv.at[n, p], at_row(1, 0, 0),
        )

    def mixed_x_then_z(slot, p):
        return remote(
            part.at[slot, 1, pl.ds(p * 128, 64), :], z_in.at[slot, p, :64, :],
            z_send.at[MIXED.index(slot) + 1], z_recv.at[slot, 0], at_row(0, DZ[p], 0),
        )

    def mixed_z_then_x(slot):
        return remote(
            x_out.at[slot, :64, :], x_in.at[slot, :64, :],
            x_send.at[1], x_recv.at[slot], at_row(1, 0, 0),
        )

    def depart(slot, group):
        if slot in MIXED and group == 0:
            for p in range(4):
                mixed_x(slot, p).start()
        else:
            for p in range(3):
                z_copy(slot, p, group).start()

    def mixed_sum(slot):
        n = MIXED.index(slot)
        for p in range(4):
            mixed_x(slot, p).wait_recv()
            part[slot, 1, p * 128 : p * 128 + 64, :] += far_in[n, p]
            if p < 3:
                mixed_x_then_z(slot, p).start()
        summed = z_total(slot, 1)
        x_out[slot, :64, :] = summed[64:]
        mixed_z_then_x(slot).start()
        total[slot, 64:, :] = summed[:64]

    def mixed_end(slot):
        mixed_z_then_x(slot).wait_recv()
        total[slot, 64:, :] += x_in[slot, :64, :]
        wait_bytes(z_recv.at[slot, 0], z_in.at[slot, :, pl.ds(0, 64), :])
        own = part[slot, 1, 384:448, :]
        total[slot, :64, :] = (own + z_in[slot, 0, :64, :]) + (
            z_in[slot, 1, :64, :] + z_in[slot, 2, :64, :]
        )
        out_copy(slot).start()

    def finish_last(slot, parts):
        load_weights(slot, parts)

        def leave(tile, carry):
            tile_product(slot, parts, False, 0, tile)
            chip_copy(slot, tile).start()
            return carry

        def keep(tile, carry):
            tile_product(slot, parts, False, 1, tile)
            chip_sum(slot, tile)
            for group in range(2):
                @pl.when(tile == group)
                def _():
                    depart(slot, group)
            return carry

        lax.fori_loop(0, 2, leave, 0)
        lax.fori_loop(0, 2, keep, 0)

    split(0, sigma_ret, sigma_less)
    begin(0, WHOLE[LESSER])
    split(1, sigma_less, None)
    own_piece.wait()
    wait_bytes(a2a_recv, advanced.at[0, pl.ds(0, 120), :])
    forward(ADVANCED, 4, 0, y_up)
    forward(ADVANCED, 2, 0, y_down)
    forward(ADVANCED, 1, 0, x_pair)
    finish(0, WHOLE[ADVANCED])
    arrived(LESSER, 2)
    begin(2, WHOLE[LESSER])
    arrived(LESSER, 4)
    begin(4, WHOLE[LESSER])
    arrived(LESSER, 1)
    forward(LESSER, 5, 1, y_up)
    forward(LESSER, 3, 1, y_down)
    forward(LESSER, 6, 4, y_up, 0)
    forward(LESSER, 6, 4, y_up, 1)
    begin(1, WHOLE[LESSER])
    arrived(ADVANCED, 2)
    forward(ADVANCED, 3, 2, x_pair, 0)
    forward(ADVANCED, 3, 2, x_pair, 1)
    forward(ADVANCED, 6, 2, y_down, 0)
    forward(ADVANCED, 6, 2, y_down, 1)
    z_sum(0)
    arrived(ADVANCED, 4)
    forward(ADVANCED, 5, 4, x_pair, 0)
    forward(ADVANCED, 5, 4, x_pair, 1)
    finish(2, WHOLE[ADVANCED])
    finish(4, WHOLE[ADVANCED])
    arrived(ADVANCED, 1)
    finish(1, WHOLE[ADVANCED])
    arrived(LESSER, 5)
    forward(LESSER, 7, 5, y_up, 0)
    forward(LESSER, 7, 5, y_up, 1)
    begin(5, WHOLE[LESSER])
    arrived(ADVANCED, 3, 0)
    forward(ADVANCED, 7, 3, y_down, 0)
    arrived(LESSER, 3)
    begin(3, WHOLE[LESSER] + ((ADVANCED, 0, 512),))
    z_sum(2)
    arrived(ADVANCED, 3, 1)
    forward(ADVANCED, 7, 3, y_down, 1)
    finish(3, ((ADVANCED, 512, 512),))
    arrived(LESSER, 6, 0)
    arrived(ADVANCED, 6, 0)
    begin(6, HALVES[0])
    arrived(LESSER, 6, 1)
    arrived(ADVANCED, 6, 1)
    finish(6, HALVES[1])
    arrived(ADVANCED, 5, 0)
    begin(5, ((ADVANCED, 0, 512),), False)
    for slot in (4, 1):
        z_sum(slot)
    arrived(LESSER, 7, 0)
    arrived(ADVANCED, 7, 0)
    begin(7, HALVES[0])
    z_sum(3)
    arrived(ADVANCED, 5, 1)
    finish(5, ((ADVANCED, 512, 512),))
    arrived(LESSER, 7, 1)
    arrived(ADVANCED, 7, 1)
    finish_last(7, HALVES[1])
    z_sum(6)
    mixed_sum(5)
    for slot in (0, 2, 4, 1):
        x_sum(slot)
    mixed_sum(7)
    x_sum(3)
    x_sum(6)
    mixed_end(5)
    mixed_end(7)

    wait_bytes(out_sem, total)
    wait_bytes(a2a_send, mirror.at[:, pl.ds(0, 15 * 1024)])
    wait_bytes(send, part.at[pl.ds(0, 7)])
    wait_bytes(chip_send, part_in)
    wait_bytes(z_send.at[0], z_in.at[pl.ds(0, 6)])
    for n in range(2):
        wait_bytes(z_send.at[n + 1], z_in.at[MIXED[n], :, pl.ds(0, 192), :])
    wait_bytes(x_send.at[0], x_out.at[pl.ds(0, 6)])
    wait_bytes(x_send.at[1], x_out.at[6])
    wait_bytes(far_send, far_in)


def on_device(sigma_ret, sigma_less, green_less, green_ret):
    dma = pltpu.SemaphoreType.DMA
    return pl.pallas_call(
        kernel,
        out_shape=jax.ShapeDtypeStruct((128, 1024), F32),
        in_specs=[pl.BlockSpec(memory_space=pltpu.HBM)] * 4,
        out_specs=pl.BlockSpec(memory_space=pl.ANY),
        scratch_shapes=[
            pltpu.VMEM((8, 1024, 128), F32),
            pltpu.VMEM((8, 128, 1024), F32),
            pltpu.VMEM((8, 16384), F32),
            pltpu.VMEM((2, 2, 1024, 1024), BF16),
            pltpu.VMEM((2, 2, 1024, 1024), BF16),
            pltpu.VMEM((AHEAD, 128, 1024), F32),
            pltpu.VMEM((1024, 256), BF16),
            pltpu.VMEM((256, 1024), BF16),
            pltpu.VMEM((8, 2, 1024, 128), F32),
            pltpu.VMEM((8, 1024, 128), F32),
            pltpu.VMEM((8, 3, 256, 128), F32),
            pltpu.VMEM((8, 128, 128), F32),
            pltpu.VMEM((8, 128, 128), F32),
            pltpu.VMEM((8, 128, 128), F32),
            dma((3,)),
            dma((AHEAD,)),
            dma(()),
            dma(()),
            dma(()),
            dma((2, 8, 2)),
            dma(()),
            dma((8, 2)),
            dma((3,)),
            dma((8, 2)),
            dma((2,)),
            dma((8,)),
            pltpu.VMEM((2, 4, 64, 128), F32),
            dma(()),
            dma((2, 4)),
            dma(()),
            pltpu.SemaphoreType.REGULAR((2,)),
        ],
        compiler_params=pltpu.CompilerParams(
            collective_id=0, has_side_effects=True, vmem_limit_bytes=53 << 20
        ),
        name="collision",
    )(sigma_ret, sigma_less, green_less, green_ret)


def solution(mesh):
    placed = (P("col", "row"), P("col", "row"), P("row", "col"), P(("col", "row"), None))
    return jax.shard_map(
        on_device, mesh=mesh, in_specs=placed, out_specs=P(("col", "row"), None), check_vma=False
    )
```

```python
import jax
import jax.numpy as jnp
from jax import lax
from jax.experimental import pallas as pl
from jax.experimental.pallas import tpu as pltpu
from jax.sharding import PartitionSpec as P

MESH = pl.DeviceIdType.MESH
F32 = jnp.float32
BF16 = jnp.bfloat16

NY, NZ = 4, 4

DY = (0, 1, 3, 2)
LESSER, ADVANCED = 0, 1
DZ = (2, 1, 3, 0)
TILE = 512
AHEAD = 8


def kernel(
    sigma_ret, sigma_less, green_less, green_ret, out,
    lesser, advanced, mirror, high, low, stage, lesser_w, advanced_w,
    part, part_in, z_in, x_out, x_in, total,
    load_sem, stage_sem, a2a_send, a2a_recv, send, recv,
    chip_send, chip_recv, z_send, z_recv, x_send, x_recv, far_in, far_send, far_recv, out_sem, ready_sem,
):
    col, row = lax.axis_index("col"), lax.axis_index("row")
    x_lo, y = col // NY, col % NY
    x_hi, z, core = row // (2 * NZ), (row // 2) % NZ, row % 2

    def at_col(dx, dy):
        return (((x_lo + dx) % 2) * NY + (y + dy) % NY, row)

    def at_row(dx, dz, dcore):
        return (col, ((x_hi + dx) % 2) * 2 * NZ + ((z + dz) % NZ) * 2 + (core + dcore) % 2)

    y_up, y_down, x_pair = at_col(0, 1), at_col(0, NY - 1), at_col(1, 0)

    load_lesser = pltpu.make_async_copy(green_less, lesser.at[0], load_sem.at[0])
    load_mirror = pltpu.make_async_copy(green_ret, mirror, load_sem.at[1])
    load_lesser.start()
    load_mirror.start()

    def stage_copy(matrix, source, t):
        half, p = t // 8, t % 8
        q = p // 2
        dz = jnp.where(q == 0, DZ[0], jnp.where(q == 1, DZ[1], jnp.where(q == 2, DZ[2], DZ[3])))
        block = at_row(p % 2, dz, 1 - half)[1]
        return pltpu.make_async_copy(
            source.at[pl.ds(pl.multiple_of(block * 128, 128), 128), :],
            stage.at[t % AHEAD],
            stage_sem.at[t % AHEAD],
        )

    for t in range(AHEAD):
        stage_copy(0, sigma_ret, t).start()

    def tell(semaphore, peers):
        for peer in peers:
            pl.semaphore_signal(semaphore, inc=1, device_id=peer, device_id_type=MESH)

    z_mates = [at_row(0, d, 0) for d in range(1, NZ)]
    near_row = [(1, 0, 0), (1, 0, 1)] + [(0, d, c) for d in (2, 1, 3) for c in (0, 1)] + [(0, 0, 1)]
    far_row = [(1, d, c) for d in (2, 1, 3) for c in (0, 1)]
    near = [y_up, y_down, x_pair] + [at_row(*place) for place in near_row]
    barrier = pltpu.get_barrier_semaphore()
    tell(barrier, near)
    pl.semaphore_wait(barrier, len(near))
    tell(ready_sem, z_mates)

    def remote(src, dst, send_sem, recv_sem, device):
        return pltpu.make_async_remote_copy(
            src_ref=src, dst_ref=dst, send_sem=send_sem, recv_sem=recv_sem,
            device_id=device, device_id_type=MESH,
        )

    panels = (lesser, advanced)

    def panel(matrix, slot, half):
        if half is None:
            return panels[matrix].at[slot]
        times = pl.ds(half * 512, 512)
        return lesser.at[slot, times, :] if matrix == LESSER else advanced.at[slot, :, times]

    def panel_copy(matrix, dst, src, device, half):
        index = (matrix, dst, half or 0)
        return remote(
            panel(matrix, src, half), panel(matrix, dst, half), send, recv.at[index], device
        )

    def forward(matrix, dst, src, device, half=None):
        copy = panel_copy(matrix, dst, src, device, half)
        copy.start()

    def arrived(matrix, slot, half=None):
        panel_copy(matrix, slot, slot, y_up, half).wait_recv()

    load_lesser.wait()
    forward(LESSER, 4, 0, y_up)
    forward(LESSER, 2, 0, y_down)

    def wait_bytes(semaphore, ref):
        pltpu.make_async_copy(ref, ref, semaphore).wait()

    mine = pl.ds(pl.multiple_of(row * 8, 8), 8)

    def columns_of(target):
        return mirror.at[:, pl.ds(pl.multiple_of(target * 1024, 1024), 1024)]

    def exchange(place):
        target = at_row(*place)
        remote(
            columns_of(target[1]), advanced.at[0, mine, :], a2a_send, a2a_recv, target
        ).start()

    load_mirror.wait()
    for place in near_row:
        exchange(place)
    own_piece = pltpu.make_async_copy(columns_of(row), advanced.at[0, mine, :], load_sem.at[2])
    own_piece.start()
    pl.semaphore_wait(ready_sem, len(z_mates))
    for place in far_row:
        exchange(place)
    forward(LESSER, 1, 0, x_pair)

    def split(matrix, source, following):
        def step(t, carry):
            stage_copy(matrix, source, t).wait()
            value = stage[t % AHEAD]
            top = value.astype(BF16)
            rest = (value - top.astype(F32)).astype(BF16)
            for group in range(2):
                rows = pl.ds(pl.multiple_of(group * 512 + (t % 8) * 64, 64), 64)
                high[matrix, t // 8, rows, :] = top[group * 64 : group * 64 + 64]
                low[matrix, t // 8, rows, :] = rest[group * 64 : group * 64 + 64]

            @pl.when(t + AHEAD < 16)
            def _():
                stage_copy(matrix, source, t + AHEAD).start()

            if following is not None:
                @pl.when(t + AHEAD >= 16)
                def _():
                    stage_copy(1, following, t + AHEAD - 16).start()
            return carry

        lax.fori_loop(0, 16, step, 0)

    MIXED = (5, 7)

    def chip_copy(slot, tile):
        rows = pl.ds(pl.multiple_of(tile * TILE, TILE), TILE)
        return remote(
            part.at[slot, 0, rows, :], part_in.at[slot, rows, :],
            chip_send, chip_recv.at[slot, tile], at_row(0, 0, 1),
        )

    def z_copy(slot, p, group):
        return remote(
            part.at[slot, 1, pl.ds(group * 512 + p * 128, 128), :],
            z_in.at[slot, p, pl.ds(group * 128, 128), :],
            z_send.at[MIXED.index(slot) + 1 if slot in MIXED else 0], z_recv.at[slot, group],
            at_row(0, DZ[p], 0),
        )

    def x_copy(slot):
        return remote(
            x_out.at[slot], x_in.at[slot], x_send.at[0], x_recv.at[slot], at_row(1, 0, 0)
        )

    def out_copy(slot):
        owner = at_col(slot % 2, DY[slot // 2])[0]
        return pltpu.make_async_copy(
            total.at[slot],
            out.at[:, pl.ds(pl.multiple_of(owner * 128, 128), 128)],
            out_sem,
        )

    def load_weights(slot, parts):
        for matrix, start, count in parts:
            times = pl.ds(start, count)
            if matrix == LESSER:
                value = lesser[slot, times, :]
                top = value.astype(BF16)
                lesser_w[times, :128] = top
                lesser_w[times, 128:] = (value - top.astype(F32)).astype(BF16)
            else:
                value = advanced[slot, :, times]
                top = value.astype(BF16)
                advanced_w[:128, times] = top
                advanced_w[128:, times] = (value - top.astype(F32)).astype(BF16)

    def tile_product(slot, parts, first, half, tile, height=TILE):
        rows = pl.ds(pl.multiple_of(tile * height, height), height)
        both = None
        for matrix, start, count in parts:
            times = pl.ds(start, count)
            if matrix == LESSER:
                weights, dims = lesser_w[times, :], (((1,), (0,)), ((), ()))
            else:
                weights, dims = advanced_w[:, times], (((1,), (1,)), ((), ()))
            for piece in (high, low):
                term = lax.dot_general(
                    piece[matrix, half, rows, times], weights, dims, preferred_element_type=F32
                )
                both = term if both is None else both + term
        both = both[:, :128] + both[:, 128:]
        if first:
            part[slot, half, rows, :] = both
        else:
            part[slot, half, rows, :] += both

    WHOLE = {LESSER: ((LESSER, 0, 1024),), ADVANCED: ((ADVANCED, 0, 1024),)}
    HALVES = [tuple((matrix, start, 512) for matrix in (LESSER, ADVANCED)) for start in (0, 512)]

    def begin(slot, parts, first=True):
        load_weights(slot, parts)

        def step(half, carry):
            tile_product(slot, parts, first, half, 0, 2 * TILE)
            return carry

        lax.fori_loop(0, 2, step, 0)

    def finish(slot, parts):
        load_weights(slot, parts)

        def step(tile, carry):
            tile_product(slot, parts, False, 0, tile)
            chip_copy(slot, tile).start()
            return carry

        lax.fori_loop(0, 2, step, 0)
        tile_product(slot, parts, False, 1, 0, 2 * TILE)
        for tile in range(2):
            chip_sum(slot, tile)
            depart(slot, tile)

    def chip_sum(slot, tile):
        rows = pl.ds(pl.multiple_of(tile * TILE, TILE), TILE)
        chip_copy(slot, tile).wait_recv()
        part[slot, 1, rows, :] += part_in[slot, rows, :]

    def z_total(slot, group):
        wait_bytes(z_recv.at[slot, group], z_in.at[slot, :, pl.ds(group * 128, 128), :])
        own = part[slot, 1, group * 512 + 384 : group * 512 + 512, :]
        rows = pl.ds(group * 128, 128)
        return (own + z_in[slot, 0, rows, :]) + (z_in[slot, 1, rows, :] + z_in[slot, 2, rows, :])

    def z_sum(slot):
        for group in range(2):
            summed = z_total(slot, group)
            rows = pl.ds(group * 64, 64)
            total[slot, rows, :] = summed[:64]
            x_out[slot, rows, :] = summed[64:]
        x_copy(slot).start()

    def x_sum(slot):
        x_copy(slot).wait_recv()
        total[slot] += x_in[slot]
        out_copy(slot).start()


    def mixed_x(slot, p):
        n = MIXED.index(slot)
        return remote(
            part.at[slot, 1, pl.ds(p * 128 + 64, 64), :], far_in.at[n, p],
            far_send, far_recv.at[n, p], at_row(1, 0, 0),
        )

    def mixed_x_then_z(slot, p):
        return remote(
            part.at[slot, 1, pl.ds(p * 128, 64), :], z_in.at[slot, p, :64, :],
            z_send.at[MIXED.index(slot) + 1], z_recv.at[slot, 0], at_row(0, DZ[p], 0),
        )

    def mixed_z_then_x(slot):
        return remote(
            x_out.at[slot, :64, :], x_in.at[slot, :64, :],
            x_send.at[1], x_recv.at[slot], at_row(1, 0, 0),
        )

    def depart(slot, group):
        if slot in MIXED and group == 0:
            for p in range(4):
                mixed_x(slot, p).start()
        else:
            for p in range(3):
                z_copy(slot, p, group).start()

    def mixed_sum(slot):
        n = MIXED.index(slot)
        for p in range(4):
            mixed_x(slot, p).wait_recv()
            part[slot, 1, p * 128 : p * 128 + 64, :] += far_in[n, p]
            if p < 3:
                mixed_x_then_z(slot, p).start()
        summed = z_total(slot, 1)
        x_out[slot, :64, :] = summed[64:]
        mixed_z_then_x(slot).start()
        total[slot, 64:, :] = summed[:64]

    def mixed_end(slot):
        mixed_z_then_x(slot).wait_recv()
        total[slot, 64:, :] += x_in[slot, :64, :]
        wait_bytes(z_recv.at[slot, 0], z_in.at[slot, :, pl.ds(0, 64), :])
        own = part[slot, 1, 384:448, :]
        total[slot, :64, :] = (own + z_in[slot, 0, :64, :]) + (
            z_in[slot, 1, :64, :] + z_in[slot, 2, :64, :]
        )
        out_copy(slot).start()

    def finish_last(slot, parts):
        load_weights(slot, parts)

        def leave(tile, carry):
            tile_product(slot, parts, False, 0, tile)
            chip_copy(slot, tile).start()
            return carry

        def keep(tile, carry):
            tile_product(slot, parts, False, 1, tile)
            chip_sum(slot, tile)
            for group in range(2):
                @pl.when(tile == group)
                def _():
                    depart(slot, group)
            return carry

        lax.fori_loop(0, 2, leave, 0)
        lax.fori_loop(0, 2, keep, 0)

    split(0, sigma_ret, sigma_less)
    begin(0, WHOLE[LESSER])
    split(1, sigma_less, None)
    own_piece.wait()
    wait_bytes(a2a_recv, advanced.at[0, pl.ds(0, 120), :])
    forward(ADVANCED, 4, 0, y_up)
    forward(ADVANCED, 2, 0, y_down)
    forward(ADVANCED, 1, 0, x_pair)
    finish(0, WHOLE[ADVANCED])
    arrived(LESSER, 2)
    begin(2, WHOLE[LESSER])
    arrived(LESSER, 4)
    begin(4, WHOLE[LESSER])
    arrived(LESSER, 1)
    forward(LESSER, 5, 1, y_up)
    forward(LESSER, 3, 1, y_down)
    forward(LESSER, 6, 4, y_up, 0)
    forward(LESSER, 6, 4, y_up, 1)
    begin(1, WHOLE[LESSER])
    arrived(ADVANCED, 2)
    forward(ADVANCED, 3, 2, x_pair, 0)
    forward(ADVANCED, 3, 2, x_pair, 1)
    forward(ADVANCED, 6, 2, y_down, 0)
    forward(ADVANCED, 6, 2, y_down, 1)
    z_sum(0)
    arrived(ADVANCED, 4)
    forward(ADVANCED, 5, 4, x_pair, 0)
    forward(ADVANCED, 5, 4, x_pair, 1)
    finish(2, WHOLE[ADVANCED])
    finish(4, WHOLE[ADVANCED])
    arrived(ADVANCED, 1)
    finish(1, WHOLE[ADVANCED])
    arrived(LESSER, 5)
    forward(LESSER, 7, 5, y_up, 0)
    forward(LESSER, 7, 5, y_up, 1)
    begin(5, WHOLE[LESSER])
    arrived(ADVANCED, 3, 0)
    forward(ADVANCED, 7, 3, y_down, 0)
    arrived(LESSER, 3)
    begin(3, WHOLE[LESSER] + ((ADVANCED, 0, 512),))
    z_sum(2)
    arrived(ADVANCED, 3, 1)
    forward(ADVANCED, 7, 3, y_down, 1)
    finish(3, ((ADVANCED, 512, 512),))
    arrived(LESSER, 6, 0)
    arrived(ADVANCED, 6, 0)
    begin(6, HALVES[0])
    arrived(LESSER, 6, 1)
    arrived(ADVANCED, 6, 1)
    finish(6, HALVES[1])
    arrived(ADVANCED, 5, 0)
    begin(5, ((ADVANCED, 0, 512),), False)
    for slot in (4, 1):
        z_sum(slot)
    arrived(LESSER, 7, 0)
    arrived(ADVANCED, 7, 0)
    begin(7, HALVES[0])
    z_sum(3)
    arrived(ADVANCED, 5, 1)
    finish(5, ((ADVANCED, 512, 512),))
    arrived(LESSER, 7, 1)
    arrived(ADVANCED, 7, 1)
    finish_last(7, HALVES[1])
    z_sum(6)
    mixed_sum(5)
    for slot in (0, 2, 4, 1):
        x_sum(slot)
    mixed_sum(7)
    x_sum(3)
    x_sum(6)
    mixed_end(5)
    mixed_end(7)

    wait_bytes(out_sem, total)
    wait_bytes(a2a_send, mirror.at[:, pl.ds(0, 15 * 1024)])
    wait_bytes(send, part.at[pl.ds(0, 7)])
    wait_bytes(chip_send, part_in)
    wait_bytes(z_send.at[0], z_in.at[pl.ds(0, 6)])
    for n in range(2):
        wait_bytes(z_send.at[n + 1], z_in.at[MIXED[n], :, pl.ds(0, 192), :])
    wait_bytes(x_send.at[0], x_out.at[pl.ds(0, 6)])
    wait_bytes(x_send.at[1], x_out.at[6])
    wait_bytes(far_send, far_in)


def on_device(sigma_ret, sigma_less, green_less, green_ret):
    dma = pltpu.SemaphoreType.DMA
    return pl.pallas_call(
        kernel,
        out_shape=jax.ShapeDtypeStruct((128, 1024), F32),
        in_specs=[pl.BlockSpec(memory_space=pltpu.HBM)] * 4,
        out_specs=pl.BlockSpec(memory_space=pl.ANY),
        scratch_shapes=[
            pltpu.VMEM((8, 1024, 128), F32),
            pltpu.VMEM((8, 128, 1024), F32),
            pltpu.VMEM((8, 16384), F32),
            pltpu.VMEM((2, 2, 1024, 1024), BF16),
            pltpu.VMEM((2, 2, 1024, 1024), BF16),
            pltpu.VMEM((AHEAD, 128, 1024), F32),
            pltpu.VMEM((1024, 256), BF16),
            pltpu.VMEM((256, 1024), BF16),
            pltpu.VMEM((8, 2, 1024, 128), F32),
            pltpu.VMEM((8, 1024, 128), F32),
            pltpu.VMEM((8, 3, 256, 128), F32),
            pltpu.VMEM((8, 128, 128), F32),
            pltpu.VMEM((8, 128, 128), F32),
            pltpu.VMEM((8, 128, 128), F32),
            dma((3,)),
            dma((AHEAD,)),
            dma(()),
            dma(()),
            dma(()),
            dma((2, 8, 2)),
            dma(()),
            dma((8, 2)),
            dma((3,)),
            dma((8, 2)),
            dma((2,)),
            dma((8,)),
            pltpu.VMEM((2, 4, 64, 128), F32),
            dma(()),
            dma((2, 4)),
            dma(()),
            pltpu.SemaphoreType.REGULAR,
        ],
        compiler_params=pltpu.CompilerParams(
            collective_id=0, has_side_effects=True, vmem_limit_bytes=53 << 20
        ),
        name="collision",
    )(sigma_ret, sigma_less, green_less, green_ret)


def solution(mesh):
    placed = (P("col", "row"), P("col", "row"), P("row", "col"), P(("col", "row"), None))
    return jax.shard_map(
        on_device, mesh=mesh, in_specs=placed, out_specs=P(("col", "row"), None), check_vma=False
    )
```

```python
import jax
import jax.numpy as jnp
from jax import lax
from jax.experimental import pallas as pl
from jax.experimental.pallas import tpu as pltpu
from jax.sharding import PartitionSpec as P

MESH = pl.DeviceIdType.MESH
F32 = jnp.float32
BF16 = jnp.bfloat16

NY, NZ = 4, 4

DY = (0, 1, 3, 2)
LESSER, ADVANCED = 0, 1
DZ = (2, 1, 3, 0)
TILE = 512
AHEAD = 8


def kernel(
    sigma_ret, sigma_less, green_less, green_ret, out,
    lesser, advanced, mirror, high, low, stage, lesser_w, advanced_w,
    part, part_in, z_in, x_out, x_in, total,
    load_sem, stage_sem, a2a_send, a2a_recv, send, recv,
    chip_send, chip_recv, z_send, z_recv, x_send, x_recv, far_in, far_send, far_recv, out_sem, ready_sem,
):
    col, row = lax.axis_index("col"), lax.axis_index("row")
    x_lo, y = col // NY, col % NY
    x_hi, z, core = row // (2 * NZ), (row // 2) % NZ, row % 2

    def at_col(dx, dy):
        return (((x_lo + dx) % 2) * NY + (y + dy) % NY, row)

    def at_row(dx, dz, dcore):
        return (col, ((x_hi + dx) % 2) * 2 * NZ + ((z + dz) % NZ) * 2 + (core + dcore) % 2)

    y_up, y_down, x_pair = at_col(0, 1), at_col(0, NY - 1), at_col(1, 0)

    def tell(semaphore, peers):
        for peer in peers:
            pl.semaphore_signal(semaphore, inc=1, device_id=peer, device_id_type=MESH)

    z_mates = [at_row(0, d, 0) for d in range(1, NZ)]
    near_row = [(1, 0, 0), (1, 0, 1)] + [(0, d, c) for d in (2, 1, 3) for c in (0, 1)] + [(0, 0, 1)]
    far_row = [(1, d, c) for d in (2, 1, 3) for c in (0, 1)]
    near = [y_up, y_down, x_pair] + [at_row(*place) for place in near_row]
    barrier = pltpu.get_barrier_semaphore()
    tell(barrier, near)

    load_lesser = pltpu.make_async_copy(green_less, lesser.at[0], load_sem.at[0])
    load_mirror = pltpu.make_async_copy(green_ret, mirror, load_sem.at[1])
    load_lesser.start()
    load_mirror.start()

    def stage_copy(matrix, source, t):
        half, p = t // 8, t % 8
        q = p // 2
        dz = jnp.where(q == 0, DZ[0], jnp.where(q == 1, DZ[1], jnp.where(q == 2, DZ[2], DZ[3])))
        block = at_row(p % 2, dz, 1 - half)[1]
        return pltpu.make_async_copy(
            source.at[pl.ds(pl.multiple_of(block * 128, 128), 128), :],
            stage.at[t % AHEAD],
            stage_sem.at[t % AHEAD],
        )

    for t in range(AHEAD):
        stage_copy(0, sigma_ret, t).start()

    pl.semaphore_wait(barrier, len(near))
    tell(ready_sem, z_mates)

    def remote(src, dst, send_sem, recv_sem, device):
        return pltpu.make_async_remote_copy(
            src_ref=src, dst_ref=dst, send_sem=send_sem, recv_sem=recv_sem,
            device_id=device, device_id_type=MESH,
        )

    panels = (lesser, advanced)

    def panel(matrix, slot, half):
        if half is None:
            return panels[matrix].at[slot]
        times = pl.ds(half * 512, 512)
        return lesser.at[slot, times, :] if matrix == LESSER else advanced.at[slot, :, times]

    def panel_copy(matrix, dst, src, device, half):
        index = (matrix, dst, half or 0)
        return remote(
            panel(matrix, src, half), panel(matrix, dst, half), send, recv.at[index], device
        )

    def forward(matrix, dst, src, device, half=None):
        copy = panel_copy(matrix, dst, src, device, half)
        copy.start()

    def arrived(matrix, slot, half=None):
        panel_copy(matrix, slot, slot, y_up, half).wait_recv()

    load_lesser.wait()
    forward(LESSER, 4, 0, y_up)
    forward(LESSER, 2, 0, y_down)

    def wait_bytes(semaphore, ref):
        pltpu.make_async_copy(ref, ref, semaphore).wait()

    mine = pl.ds(pl.multiple_of(row * 8, 8), 8)

    def columns_of(target):
        return mirror.at[:, pl.ds(pl.multiple_of(target * 1024, 1024), 1024)]

    def exchange(place):
        target = at_row(*place)
        remote(
            columns_of(target[1]), advanced.at[0, mine, :], a2a_send, a2a_recv, target
        ).start()

    load_mirror.wait()
    for place in near_row:
        exchange(place)
    own_piece = pltpu.make_async_copy(columns_of(row), advanced.at[0, mine, :], load_sem.at[2])
    own_piece.start()
    pl.semaphore_wait(ready_sem, len(z_mates))
    for place in far_row:
        exchange(place)
    forward(LESSER, 1, 0, x_pair)

    def split(matrix, source, following):
        def step(t, carry):
            stage_copy(matrix, source, t).wait()
            value = stage[t % AHEAD]
            top = value.astype(BF16)
            rest = (value - top.astype(F32)).astype(BF16)
            for group in range(2):
                rows = pl.ds(pl.multiple_of(group * 512 + (t % 8) * 64, 64), 64)
                high[matrix, t // 8, rows, :] = top[group * 64 : group * 64 + 64]
                low[matrix, t // 8, rows, :] = rest[group * 64 : group * 64 + 64]

            @pl.when(t + AHEAD < 16)
            def _():
                stage_copy(matrix, source, t + AHEAD).start()

            if following is not None:
                @pl.when(t + AHEAD >= 16)
                def _():
                    stage_copy(1, following, t + AHEAD - 16).start()
            return carry

        lax.fori_loop(0, 16, step, 0)

    MIXED = (5, 7)

    def chip_copy(slot, tile):
        rows = pl.ds(pl.multiple_of(tile * TILE, TILE), TILE)
        return remote(
            part.at[slot, 0, rows, :], part_in.at[slot, rows, :],
            chip_send, chip_recv.at[slot, tile], at_row(0, 0, 1),
        )

    def z_copy(slot, p, group):
        return remote(
            part.at[slot, 1, pl.ds(group * 512 + p * 128, 128), :],
            z_in.at[slot, p, pl.ds(group * 128, 128), :],
            z_send.at[MIXED.index(slot) + 1 if slot in MIXED else 0], z_recv.at[slot, group],
            at_row(0, DZ[p], 0),
        )

    def x_copy(slot):
        return remote(
            x_out.at[slot], x_in.at[slot], x_send.at[0], x_recv.at[slot], at_row(1, 0, 0)
        )

    def out_copy(slot):
        owner = at_col(slot % 2, DY[slot // 2])[0]
        return pltpu.make_async_copy(
            total.at[slot],
            out.at[:, pl.ds(pl.multiple_of(owner * 128, 128), 128)],
            out_sem,
        )

    def load_weights(slot, parts):
        for matrix, start, count in parts:
            times = pl.ds(start, count)
            if matrix == LESSER:
                value = lesser[slot, times, :]
                top = value.astype(BF16)
                lesser_w[times, :128] = top
                lesser_w[times, 128:] = (value - top.astype(F32)).astype(BF16)
            else:
                value = advanced[slot, :, times]
                top = value.astype(BF16)
                advanced_w[:128, times] = top
                advanced_w[128:, times] = (value - top.astype(F32)).astype(BF16)

    def tile_product(slot, parts, first, half, tile, height=TILE):
        rows = pl.ds(pl.multiple_of(tile * height, height), height)
        both = None
        for matrix, start, count in parts:
            times = pl.ds(start, count)
            if matrix == LESSER:
                weights, dims = lesser_w[times, :], (((1,), (0,)), ((), ()))
            else:
                weights, dims = advanced_w[:, times], (((1,), (1,)), ((), ()))
            for piece in (high, low):
                term = lax.dot_general(
                    piece[matrix, half, rows, times], weights, dims, preferred_element_type=F32
                )
                both = term if both is None else both + term
        both = both[:, :128] + both[:, 128:]
        if first:
            part[slot, half, rows, :] = both
        else:
            part[slot, half, rows, :] += both

    WHOLE = {LESSER: ((LESSER, 0, 1024),), ADVANCED: ((ADVANCED, 0, 1024),)}
    HALVES = [tuple((matrix, start, 512) for matrix in (LESSER, ADVANCED)) for start in (0, 512)]

    def begin(slot, parts, first=True):
        load_weights(slot, parts)

        def step(half, carry):
            tile_product(slot, parts, first, half, 0, 2 * TILE)
            return carry

        lax.fori_loop(0, 2, step, 0)

    def finish(slot, parts):
        load_weights(slot, parts)

        def step(tile, carry):
            tile_product(slot, parts, False, 0, tile)
            chip_copy(slot, tile).start()
            return carry

        lax.fori_loop(0, 2, step, 0)
        tile_product(slot, parts, False, 1, 0, 2 * TILE)
        for tile in range(2):
            chip_sum(slot, tile)
            depart(slot, tile)

    def chip_sum(slot, tile):
        rows = pl.ds(pl.multiple_of(tile * TILE, TILE), TILE)
        chip_copy(slot, tile).wait_recv()
        part[slot, 1, rows, :] += part_in[slot, rows, :]

    def z_total(slot, group):
        wait_bytes(z_recv.at[slot, group], z_in.at[slot, :, pl.ds(group * 128, 128), :])
        own = part[slot, 1, group * 512 + 384 : group * 512 + 512, :]
        rows = pl.ds(group * 128, 128)
        return (own + z_in[slot, 0, rows, :]) + (z_in[slot, 1, rows, :] + z_in[slot, 2, rows, :])

    def z_sum(slot):
        for group in range(2):
            summed = z_total(slot, group)
            rows = pl.ds(group * 64, 64)
            total[slot, rows, :] = summed[:64]
            x_out[slot, rows, :] = summed[64:]
        x_copy(slot).start()

    def x_sum(slot):
        x_copy(slot).wait_recv()
        total[slot] += x_in[slot]
        out_copy(slot).start()


    def mixed_x(slot, p):
        n = MIXED.index(slot)
        return remote(
            part.at[slot, 1, pl.ds(p * 128 + 64, 64), :], far_in.at[n, p],
            far_send, far_recv.at[n, p], at_row(1, 0, 0),
        )

    def mixed_x_then_z(slot, p):
        return remote(
            part.at[slot, 1, pl.ds(p * 128, 64), :], z_in.at[slot, p, :64, :],
            z_send.at[MIXED.index(slot) + 1], z_recv.at[slot, 0], at_row(0, DZ[p], 0),
        )

    def mixed_z_then_x(slot):
        return remote(
            x_out.at[slot, :64, :], x_in.at[slot, :64, :],
            x_send.at[1], x_recv.at[slot], at_row(1, 0, 0),
        )

    def depart(slot, group):
        if slot in MIXED and group == 0:
            for p in range(4):
                mixed_x(slot, p).start()
        else:
            for p in range(3):
                z_copy(slot, p, group).start()

    def mixed_sum(slot):
        n = MIXED.index(slot)
        for p in range(4):
            mixed_x(slot, p).wait_recv()
            part[slot, 1, p * 128 : p * 128 + 64, :] += far_in[n, p]
            if p < 3:
                mixed_x_then_z(slot, p).start()
        summed = z_total(slot, 1)
        x_out[slot, :64, :] = summed[64:]
        mixed_z_then_x(slot).start()
        total[slot, 64:, :] = summed[:64]

    def mixed_end(slot):
        mixed_z_then_x(slot).wait_recv()
        total[slot, 64:, :] += x_in[slot, :64, :]
        wait_bytes(z_recv.at[slot, 0], z_in.at[slot, :, pl.ds(0, 64), :])
        own = part[slot, 1, 384:448, :]
        total[slot, :64, :] = (own + z_in[slot, 0, :64, :]) + (
            z_in[slot, 1, :64, :] + z_in[slot, 2, :64, :]
        )
        out_copy(slot).start()

    def finish_last(slot, parts):
        load_weights(slot, parts)

        def leave(tile, carry):
            tile_product(slot, parts, False, 0, tile)
            chip_copy(slot, tile).start()
            return carry

        def keep(tile, carry):
            tile_product(slot, parts, False, 1, tile)
            chip_sum(slot, tile)
            for group in range(2):
                @pl.when(tile == group)
                def _():
                    depart(slot, group)
            return carry

        lax.fori_loop(0, 2, leave, 0)
        lax.fori_loop(0, 2, keep, 0)

    split(0, sigma_ret, sigma_less)
    begin(0, WHOLE[LESSER])
    split(1, sigma_less, None)
    own_piece.wait()
    wait_bytes(a2a_recv, advanced.at[0, pl.ds(0, 120), :])
    forward(ADVANCED, 4, 0, y_up)
    forward(ADVANCED, 2, 0, y_down)
    forward(ADVANCED, 1, 0, x_pair)
    finish(0, WHOLE[ADVANCED])
    arrived(LESSER, 2)
    begin(2, WHOLE[LESSER])
    arrived(LESSER, 4)
    begin(4, WHOLE[LESSER])
    arrived(LESSER, 1)
    forward(LESSER, 5, 1, y_up)
    forward(LESSER, 3, 1, y_down)
    forward(LESSER, 6, 4, y_up, 0)
    forward(LESSER, 6, 4, y_up, 1)
    begin(1, WHOLE[LESSER])
    arrived(ADVANCED, 2)
    forward(ADVANCED, 3, 2, x_pair, 0)
    forward(ADVANCED, 3, 2, x_pair, 1)
    forward(ADVANCED, 6, 2, y_down, 0)
    forward(ADVANCED, 6, 2, y_down, 1)
    z_sum(0)
    arrived(ADVANCED, 4)
    forward(ADVANCED, 5, 4, x_pair, 0)
    forward(ADVANCED, 5, 4, x_pair, 1)
    finish(2, WHOLE[ADVANCED])
    finish(4, WHOLE[ADVANCED])
    arrived(ADVANCED, 1)
    finish(1, WHOLE[ADVANCED])
    arrived(LESSER, 5)
    forward(LESSER, 7, 5, y_up, 0)
    forward(LESSER, 7, 5, y_up, 1)
    begin(5, WHOLE[LESSER])
    arrived(ADVANCED, 3, 0)
    forward(ADVANCED, 7, 3, y_down, 0)
    arrived(LESSER, 3)
    begin(3, WHOLE[LESSER] + ((ADVANCED, 0, 512),))
    z_sum(2)
    arrived(ADVANCED, 3, 1)
    forward(ADVANCED, 7, 3, y_down, 1)
    finish(3, ((ADVANCED, 512, 512),))
    arrived(LESSER, 6, 0)
    arrived(ADVANCED, 6, 0)
    begin(6, HALVES[0])
    arrived(LESSER, 6, 1)
    arrived(ADVANCED, 6, 1)
    finish(6, HALVES[1])
    arrived(ADVANCED, 5, 0)
    begin(5, ((ADVANCED, 0, 512),), False)
    for slot in (4, 1):
        z_sum(slot)
    arrived(LESSER, 7, 0)
    arrived(ADVANCED, 7, 0)
    begin(7, HALVES[0])
    z_sum(3)
    arrived(ADVANCED, 5, 1)
    finish(5, ((ADVANCED, 512, 512),))
    arrived(LESSER, 7, 1)
    arrived(ADVANCED, 7, 1)
    finish_last(7, HALVES[1])
    z_sum(6)
    mixed_sum(5)
    for slot in (0, 2, 4, 1):
        x_sum(slot)
    mixed_sum(7)
    x_sum(3)
    x_sum(6)
    mixed_end(5)
    mixed_end(7)

    wait_bytes(out_sem, total)
    wait_bytes(a2a_send, mirror.at[:, pl.ds(0, 15 * 1024)])
    wait_bytes(send, part.at[pl.ds(0, 7)])
    wait_bytes(chip_send, part_in)
    wait_bytes(z_send.at[0], z_in.at[pl.ds(0, 6)])
    for n in range(2):
        wait_bytes(z_send.at[n + 1], z_in.at[MIXED[n], :, pl.ds(0, 192), :])
    wait_bytes(x_send.at[0], x_out.at[pl.ds(0, 6)])
    wait_bytes(x_send.at[1], x_out.at[6])
    wait_bytes(far_send, far_in)


def on_device(sigma_ret, sigma_less, green_less, green_ret):
    dma = pltpu.SemaphoreType.DMA
    return pl.pallas_call(
        kernel,
        out_shape=jax.ShapeDtypeStruct((128, 1024), F32),
        in_specs=[pl.BlockSpec(memory_space=pltpu.HBM)] * 4,
        out_specs=pl.BlockSpec(memory_space=pl.ANY),
        scratch_shapes=[
            pltpu.VMEM((8, 1024, 128), F32),
            pltpu.VMEM((8, 128, 1024), F32),
            pltpu.VMEM((8, 16384), F32),
            pltpu.VMEM((2, 2, 1024, 1024), BF16),
            pltpu.VMEM((2, 2, 1024, 1024), BF16),
            pltpu.VMEM((AHEAD, 128, 1024), F32),
            pltpu.VMEM((1024, 256), BF16),
            pltpu.VMEM((256, 1024), BF16),
            pltpu.VMEM((8, 2, 1024, 128), F32),
            pltpu.VMEM((8, 1024, 128), F32),
            pltpu.VMEM((8, 3, 256, 128), F32),
            pltpu.VMEM((8, 128, 128), F32),
            pltpu.VMEM((8, 128, 128), F32),
            pltpu.VMEM((8, 128, 128), F32),
            dma((3,)),
            dma((AHEAD,)),
            dma(()),
            dma(()),
            dma(()),
            dma((2, 8, 2)),
            dma(()),
            dma((8, 2)),
            dma((3,)),
            dma((8, 2)),
            dma((2,)),
            dma((8,)),
            pltpu.VMEM((2, 4, 64, 128), F32),
            dma(()),
            dma((2, 4)),
            dma(()),
            pltpu.SemaphoreType.REGULAR,
        ],
        compiler_params=pltpu.CompilerParams(
            collective_id=0, has_side_effects=True, vmem_limit_bytes=53 << 20
        ),
        name="collision",
    )(sigma_ret, sigma_less, green_less, green_ret)


def solution(mesh):
    placed = (P("col", "row"), P("col", "row"), P("row", "col"), P(("col", "row"), None))
    return jax.shard_map(
        on_device, mesh=mesh, in_specs=placed, out_specs=P(("col", "row"), None), check_vma=False
    )
```
